32 devices in a mesh: traj: 4 (over z), lon: 8 (over y, x, core).
Axes of the slice: x: 2, y: 2, z: 4, core: 2. Of those that a mesh axis runs over, the one named last changes fastest.
Arguments:
- states: float32 [4, 78, 16, 1024], P('traj', None, None, 'lon')
- obs_index: int32 [4, 2048], P('traj', 'lon'), may hold values from 0 to 16383, as said below
- obs_values: float32 [4, 78, 2048], P('traj', None, 'lon'), may hold values from -8 to 8
- first_weight: bfloat16 [256, 2106], replicated, may hold values from -0.125 to 0.125
- first_bias: float32 [256], replicated, may hold values from -4 to 4
- second_weight: bfloat16 [234, 2304], replicated, may hold values from -0.125 to 0.125
Outputs:
- updated: float32 [4, 78, 16, 1024], P('traj', None, None, 'lon')
The draws below stay inside these ranges and needn't reach their ends.
Inputs may be any that keep to these rules, and one draw needn't show every extreme that they name: Entries k of obs_index[t] with k // 256 = j lie in longitude columns j * 128 to (j + 1) * 128 - 1; the cells of one state are distinct.
All inputs are finite; a program needn't handle non-finite values.
Results may differ from the reference program's by a relative error of at most 0.0028.
Values may be sent and summed in bfloat16 or wider, within the bound.
A program may use at most 128 MiB of HBM per device.

```python
import jax
import jax.numpy as jnp
from jax import lax

VARS = 78
HIDDEN_W = 256
LAT = 16
LON_DEV = 128
NOBS = 256
STEPS = 2
STATES = 4
LON = 1024
NOBS_ALL = 2048


def draw_states(key, part):
    base_key, var_key = jax.random.split(jax.random.fold_in(key, 11))
    base = jax.random.normal(base_key, (STATES, VARS, LAT, LON), jnp.float32)
    var_scale = jnp.exp(jax.random.uniform(var_key, (VARS,), jnp.float32, jnp.log(0.3), jnp.log(3.0)))
    state_scale = 1.0 + 0.35 * jnp.arange(STATES, dtype=jnp.float32) / max(STATES - 1, 1)
    lon_scale = 1.0 + 0.35 * jnp.arange(LON, dtype=jnp.float32) / LON
    field = base * var_scale[None, :, None, None] * state_scale[:, None, None, None] * lon_scale[None, None, None, :]
    return 0.3 * field


def draw_obs_index(key, part):
    bands = LON // LON_DEV
    keys = jax.random.split(jax.random.fold_in(key, 23), STATES * bands)
    chosen = jax.vmap(lambda k: jax.random.permutation(k, LAT * LON_DEV)[:NOBS])(keys)
    chosen = chosen.reshape(STATES, bands, NOBS).astype(jnp.int32)
    band = jnp.arange(bands, dtype=jnp.int32)[None, :, None]
    row = chosen // LON_DEV
    column = chosen % LON_DEV
    cell = row * LON + band * LON_DEV + column
    return cell.reshape(STATES, bands * NOBS).astype(jnp.int32)


def levels(own_key, dims, cuts, least, top_value):
    gain, own = 1.0, jax.random.fold_in(own_key, 6)
    for axis_at, parts in cuts:
        draws = jnp.exp(jax.random.uniform(jax.random.fold_in(own, axis_at), (parts,), jnp.float32, least / len(cuts), top_value / len(cuts)))
        gain = gain * jnp.repeat(draws, dims[axis_at] // parts).reshape([-1 if axis == axis_at else 1 for axis in range(len(dims))])
    return gain


def centred(key, dims, width, bound, cuts=(), kind=jnp.bfloat16):
    level = levels(key, dims, cuts, -0.22, 0.18) if cuts else 1.0
    entries = jax.random.normal(key, dims, jnp.float32) * width * level
    return jnp.minimum(jnp.maximum(entries, -bound), bound).astype(kind)


def setup_inputs(seed: int = 0) -> dict:
    arg_keys = jax.random.split(jax.random.key(seed), 7)
    states = draw_states(jax.random.fold_in(arg_keys[6], 71), 0)
    obs_index = draw_obs_index(jax.random.fold_in(arg_keys[6], 71), 0)
    obs_values = centred(arg_keys[2], (STATES, VARS, NOBS_ALL), 1.5, 8.0, ((0, 4), (2, 8)), jnp.float32)
    first_weight = centred(arg_keys[3], (HIDDEN_W, 27 * VARS), (27 * VARS) ** -0.5, 0.125)
    first_bias = centred(arg_keys[4], (HIDDEN_W,), 0.7, 4.0, (), jnp.float32)
    second_weight = centred(arg_keys[5], (3 * VARS, 9 * HIDDEN_W), (9 * HIDDEN_W) ** -0.5, 0.125)
    return {"states": states, "obs_index": obs_index, "obs_values": obs_values, "first_weight": first_weight, "first_bias": first_bias, "second_weight": second_weight}


def make_patches(padded, rows, cols):
    pieces = [padded[:, a:a + rows, b:b + cols] for a in range(3) for b in range(3)]
    stacked = jnp.stack(pieces, 0)
    return stacked.reshape(stacked.shape[0] * stacked.shape[1], rows * cols)

def pad_field(field):
    wrapped = jnp.concatenate([field[:, :, -1:], field, field[:, :, :1]], 2)
    return jnp.pad(wrapped, ((0, 0), (1, 1), (0, 0)))

def network(window, first_weight, first_bias, second_weight):
    rows = window.shape[1]
    cols = window.shape[2]
    patches = make_patches(pad_field(window), rows, cols)
    hidden = jnp.dot(first_weight, patches, preferred_element_type=jnp.float32) + first_bias[:, None]
    hidden = jax.nn.silu(hidden).astype(jnp.bfloat16).reshape(-1, rows, cols)
    patches = make_patches(pad_field(hidden), rows, cols)
    return jnp.dot(second_weight, patches, preferred_element_type=jnp.float32).reshape(-1, rows, cols)

def reference(states, obs_index, obs_values, first_weight, first_bias, second_weight):
    nvar = states.shape[1]
    rows = states.shape[2]
    cols = states.shape[3]
    count = states.shape[0] * rows * cols
    x = states
    for step in range(STEPS):
        moment = lax.optimization_barrier(jnp.sum(x * x, axis=(0, 2, 3))) / count
        scale = 1.0 / jnp.sqrt(moment + 1e-06)
        normed = (x * scale[None, :, None, None]).astype(jnp.bfloat16)
        blank = jnp.zeros_like(normed[:1])
        before = jnp.concatenate([blank, normed[:-1]], 0)
        after = jnp.concatenate([normed[1:], blank], 0)
        windows = jnp.concatenate([before, normed, after], 1)
        contrib = lax.map(lambda w: network(w, first_weight, first_bias, second_weight), windows)
        zero_part = jnp.zeros_like(contrib[:1, :nvar])
        score = contrib[:, nvar:2 * nvar]
        score = score + jnp.concatenate([zero_part, contrib[:-1, 2 * nvar:]], 0)
        score = score + jnp.concatenate([contrib[1:, :nvar], zero_part], 0)
        flat = x.reshape(x.shape[0], nvar, rows * cols)

        def guide_one(field, index, values):
            seen = field[:, index]
            return jnp.zeros_like(field).at[:, index].add(values - seen)
        guide = jax.vmap(guide_one)(flat, obs_index, obs_values).reshape(x.shape)
        x = x + 0.5 * (score + guide)
    return x
```

```python
import functools

import jax
import jax.numpy as jnp
from jax import lax
from jax.experimental import pallas as pl
from jax.experimental.pallas import tpu as pltpu
from jax.sharding import PartitionSpec as P

STEPS = 2
F32 = jnp.float32
BF16 = jnp.bfloat16
LANES = 128
HALF = 64
PIECE = 16
MESH = pl.DeviceIdType.MESH


def lane_of(shape):
    return lax.broadcasted_iota(jnp.int32, shape, len(shape) - 1)


def turned(value, by):
    by = by % LANES
    return value if by == 0 else pltpu.roll(value, by, len(value.shape) - 1)


def pack_pair(lane, low, high):
    return jnp.where(lane < HALF, low, turned(high, HALF))


def pack_tails(lane, cols):
    out = jnp.zeros_like(cols[0])
    for i, col in enumerate(cols):
        out = jnp.where(lane // PIECE == i, turned(col, PIECE * i - HALF), out)
    return out


def kernel(
    nt, nl, nvar, rows, cols, hid,
    x_ref, loc_ref, val_ref, w1_ref, b1_ref, w2_ref, out_ref,
    xn, xt, base, quot, obs3, bt, pn, pb, rn, rb, en, eb, nu, xb, x3, acc, h3, score,
    qs, rq, st, red1, sum1, red2,
    bar_n_s, bar_n_r, bar_b_s, bar_b_r, edge_s, edge_n_r, edge_b_r, ret_s, ret_r,
    r1_s, r1_r, r2_s, r2_r,
):
    t = lax.axis_index("traj")
    b = lax.axis_index("lon")
    cw = cols // nt
    halo = 2 * STEPS
    ext = cw + 2 * halo
    mt = 5 * cw // 8
    tiles = mt + 6
    count = nt * rows * cols * nl
    lane = lane_of((rows, LANES))
    row = lax.broadcasted_iota(jnp.int32, (rows, LANES), 0)

    def dev(tt, bb):
        return {"traj": lax.rem(tt, nt), "lon": lax.rem(bb, nl)}

    barrier = pltpu.get_barrier_semaphore()
    partners = 0
    for db in range(nl):
        for dt in range(nt):
            near = db in (0, 1, nl - 1)
            if (db or dt) and (near or dt == 0):
                pl.semaphore_signal(barrier, inc=1, device_id=dev(t + dt, b + db), device_id_type=MESH)
                partners += 1

    xn[0 : nvar * rows, :] = x_ref[...]
    xn[nvar * rows :, :] = jnp.zeros((LANES * rows - nvar * rows, LANES), F32)

    def flip(r, c):
        xt[pl.ds(r, cols, stride=rows), :] = xn[pl.ds(r, LANES, stride=rows), :].T
        return c

    lax.fori_loop(0, rows, flip, 0)

    def squares(ref, first, n):
        def one(i, c):
            v = ref[pl.ds(first + i * 32, 32), :]
            return c + v * v

        s = lax.fori_loop(0, n // 32, one, jnp.zeros((32, LANES), F32))
        return s[0:8] + s[8:16] + s[16:24] + s[24:32]

    def reduced(step, part, first):
        sum1[step, 0] = part
        copies = []
        for i in range(1, nt):
            cp = pltpu.make_async_remote_copy(
                sum1.at[step, 0], red1.at[step, i], r1_s.at[step, i], r1_r.at[step, i],
                device_id=dev(t + i, b), device_id_type=MESH)
            cp.start()
            copies.append(cp)
        tot = part
        for i in range(1, nt):
            copies[i - 1].wait()
            tot = tot + red1[step, i]
        sum1[step, 1] = tot
        copies = []
        for i in range(1, nl):
            cp = pltpu.make_async_remote_copy(
                sum1.at[step, 1], red2.at[step, i], r2_s.at[step, i], r2_r.at[step, i],
                device_id=dev(t, b + i), device_id_type=MESH)
            cp.start()
            copies.append(cp)
        for i in range(1, nl):
            copies[i - 1].wait()
            tot = tot + red2[step, i]
        moment = jnp.sum(tot, axis=0, keepdims=True) / count
        return jnp.broadcast_to(1.0 / jnp.sqrt(moment + 1e-06), (rows, LANES))

    part = squares(xt, 0, cols * rows)
    pl.semaphore_wait(barrier, partners)
    scale = reduced(0, part, True)

    def pack_all(get, dest):
        zero = jnp.zeros((3, rows, LANES), BF16)
        dest[1, 0:3] = zero
        dest[nt, tiles - 3 :] = zero

        def sub(k, carry):
            def pair(j, c):
                dest[k + 1, 3 + j] = pack_pair(lane, get(k * cw + j), get(k * cw + j + cw // 2)).astype(BF16)
                return c

            lax.fori_loop(0, cw // 2, pair, 0, unroll=2)

            def tail(j, c):
                dest[k + 1, 3 + cw // 2 + j] = pack_tails(
                    lane, [get(k * cw + j + cw // 8 * i) for i in range(8)]).astype(BF16)
                return c

            lax.fori_loop(0, cw // 8, tail, 0)
            for first, slot, at in ((k * cw, k, tiles - 3), (k * cw + cw - halo, k + 2, 0)):
                four = [get(first + i) for i in range(4)]
                dest[slot, at] = pack_pair(lane, four[0], four[2]).astype(BF16)
                dest[slot, at + 1] = pack_pair(lane, four[1], four[3]).astype(BF16)
                dest[slot, at + 2] = pack_tails(lane, four).astype(BF16)
            return carry

        lax.fori_loop(0, nt, sub, 0)

    def send_all(src, dst, edge, s_sem, r_sem, e_sem, f):
        copies = []
        for i in range(1, nt):
            k = lax.rem(t + i, nt)
            cp = pltpu.make_async_remote_copy(
                src.at[k + 1], dst.at[t], s_sem.at[i], r_sem.at[t],
                device_id=dev(k, b), device_id_type=MESH)
            cp.start()
            copies.append(cp)
        right = pltpu.make_async_remote_copy(
            src.at[nt + 1, 0:3], edge.at[t], edge_s.at[f, 0], e_sem.at[t],
            device_id=dev(0, b + 1), device_id_type=MESH)
        left = pltpu.make_async_remote_copy(
            src.at[0, tiles - 3 : tiles], edge.at[t], edge_s.at[f, 1], e_sem.at[t],
            device_id=dev(nt - 1, b + nl - 1), device_id_type=MESH)
        right.start()
        left.start()
        dst[t] = src[t + 1]
        return copies + [right, left]

    def receive(src, dst, edge, s_sem, r_sem, e_sem, f):
        for i in range(1, nt):
            k = lax.rem(t + i, nt)
            pltpu.make_async_remote_copy(
                src.at[k + 1], dst.at[k], s_sem.at[i], r_sem.at[k],
                device_id=dev(k, b), device_id_type=MESH).wait_recv()

        def edges(at, side):
            for k in range(nt):
                pltpu.make_async_remote_copy(
                    src.at[0, 0:3], edge.at[k], edge_s.at[f, 0], e_sem.at[k],
                    device_id=dev(0, b + 1), device_id_type=MESH).wait_recv()
                dst[k, at : at + 3] = edge[k]

        @pl.when(t == 0)
        def _():
            edges(0, 1)

        @pl.when(t == nt - 1)
        def _():
            edges(tiles - 3, -1)

    def unpack_all(src, put):
        def state(s, carry):
            def tile(j):
                return src[s, j].astype(F32)

            for at, first in ((0, 0), (tiles - 3, cw + halo)):
                pairs = [tile(at), tile(at + 1)]
                tail = tile(at + 2)
                for i in range(4):
                    a = turned(pairs[i % 2], HALF * (i // 2))
                    put(s, first + i, jnp.where(lane < HALF, a, turned(tail, HALF - PIECE * i)))
            unpack_main(lambda j: tile(3 + j), lambda c, v: put(s, c + halo, v))
            return carry

        lax.fori_loop(0, nt, state, 0)

    def unpack_main(tile, put):
        for i in range(8):
            def one(j, c, i=i):
                at = i * (cw // 8) + j
                a = turned(tile(at % (cw // 2) if isinstance(at, int) else at - (i // 4) * (cw // 2)), HALF * (i // 4))
                put(at, jnp.where(lane < HALF, a, turned(tile(cw // 2 + j), HALF - PIECE * i)))
                return c

            lax.fori_loop(0, cw // 8, one, 0, unroll=2)

    pack_all(lambda c: xt[pl.ds(c * rows, rows), :] * scale, pn)
    sent_n = send_all(pn, rn, en, bar_n_s, bar_n_r, edge_n_r, 0)

    vals = jnp.concatenate([val_ref[...], jnp.ones((8, val_ref.shape[1]), F32)], 0) if nvar % 8 == 0 else None
    if vals is None:
        obs_rows = val_ref.shape[0]
        obs3[0, 0:obs_rows] = val_ref[...]
        obs3[0, obs_rows:] = jnp.ones((LANES - obs_rows, val_ref.shape[1]), F32)
    else:
        obs3[0, 0 : nvar + 8] = vals
        obs3[0, nvar + 8 :] = jnp.zeros((LANES - nvar - 8, val_ref.shape[1]), F32)
    full = obs3[0]
    high = full.astype(BF16)
    rest = full - high.astype(F32)
    mid = rest.astype(BF16)
    low = (rest - mid.astype(F32)).astype(BF16)
    three = jnp.concatenate([high, mid, low], 0)
    loc = loc_ref[...]

    def observe(r, c):
        cell = lax.broadcasted_iota(jnp.int32, (cols, loc.shape[1]), 0) + r * cols
        hot = jnp.where(cell == loc, 1.0, 0.0).astype(BF16)
        o = lax.dot_general(three, hot, (((1,), (1,)), ((), ())), preferred_element_type=F32)
        o = o[0:LANES] + o[LANES : 2 * LANES] + o[2 * LANES :]
        seen = o[nvar : nvar + 1, :] > 0.5
        x = xn[pl.ds(r, LANES, stride=rows), :]
        g = jnp.where(seen, 0.5 * (o - x), 0.0)
        base[pl.ds(r, LANES, stride=rows), :] = jnp.where(seen, 0.5 * (x + g + o), x)
        quot[pl.ds(r, 1), :] = jnp.where(seen, 0.25, 0.5)
        bt[pl.ds(r, cols, stride=rows), :] = (x + g).T
        return c

    lax.fori_loop(0, rows, observe, 0)
    pack_all(lambda c: bt[pl.ds(c * rows, rows), :], pb)
    sent_b = send_all(pb, rb, eb, bar_b_s, bar_b_r, edge_b_r, 1)

    nu[0] = jnp.zeros(nu.shape[1:], F32)
    nu[nt + 1] = jnp.zeros(nu.shape[1:], F32)
    receive(pn, rn, en, bar_n_s, bar_n_r, edge_n_r, 0)

    def put_n(s, c, v):
        nu[s + 1, c] = v

    unpack_all(rn, put_n)

    def spread(dest, c, tile_list):
        n = len(tile_list)
        for i, v in enumerate(tile_list):
            up = jnp.where(row == 0, 0.0, pltpu.roll(v, 1, 0))
            down = jnp.where(row == rows - 1, 0.0, pltpu.roll(v, rows - 1, 0))
            for a, piece in enumerate((up, v, down)):
                dest[c, :, a * n * LANES + i * LANES : a * n * LANES + (i + 1) * LANES] = piece.astype(BF16)

    wide = 2 * LANES
    two = 2 * nvar - LANES

    def network(width):
        score[...] = jnp.zeros(score.shape, F32)

        def state(s, carry):
            def window(c, k):
                before, here, after = nu[s, c], nu[s + 1, c], nu[s + 2, c]
                moved = turned(here, nvar)
                first = jnp.where(lane < nvar, before, moved)
                last = jnp.where(lane < two, moved, jnp.where(lane < two + nvar, turned(after, two), 0.0))
                spread(x3, c, [first, last])
                return k

            lax.fori_loop(0, width, window, 0, unroll=2)
            wid = width - 2
            lhs = jnp.concatenate(
                [x3[i : i + wid].reshape(wid * rows, 3 * wide) for i in range(3)], 1)
            acc[0 : wid * rows, :] = jnp.dot(lhs, w1_ref[...], preferred_element_type=F32)
            bias = jnp.broadcast_to(b1_ref[...], (rows, hid))

            def activate(c, k):
                v = acc[pl.ds(c * rows, rows), :] + bias
                v = v / (1.0 + jnp.exp(-v))
                v = v.astype(BF16).astype(F32)
                spread(h3, c, [v[:, i * LANES : (i + 1) * LANES] for i in range(hid // LANES)])
                return k

            lax.fori_loop(0, wid, activate, 0, unroll=2)
            wid = width - 4
            lhs = jnp.concatenate(
                [h3[i : i + wid].reshape(wid * rows, 3 * hid) for i in range(3)], 1)
            acc[0 : wid * rows, :] = jnp.dot(lhs, w2_ref[...], preferred_element_type=F32)

            def share(c, k):
                c0 = acc[pl.ds(c * rows, rows), 0:LANES]
                c1 = acc[pl.ds(c * rows, rows), LANES : 2 * LANES]
                mid_part = jnp.where(lane < LANES - nvar, turned(c0, -nvar), turned(c1, -nvar))
                score[s, c] += c0
                score[s + 1, c] += mid_part
                score[s + 2, c] += turned(c1, -two)
                return k

            lax.fori_loop(0, wid, share, 0, unroll=2)
            return carry

        lax.fori_loop(0, nt, state, 0)

    def give_back(step, off):
        def state(s, carry):
            def get(c):
                return score[s + 1, c + off]

            def pair(j, c):
                qs[step, s, j] = pack_pair(lane, get(j), get(j + cw // 2)).astype(BF16)
                return c

            lax.fori_loop(0, cw // 2, pair, 0, unroll=2)

            def tail(j, c):
                qs[step, s, cw // 2 + j] = pack_tails(
                    lane, [get(j + cw // 8 * i) for i in range(8)]).astype(BF16)
                return c

            lax.fori_loop(0, cw // 8, tail, 0)
            return carry

        lax.fori_loop(0, nt, state, 0)
        copies = []
        for i in range(1, nt):
            k = lax.rem(t + i, nt)
            cp = pltpu.make_async_remote_copy(
                qs.at[step, k], rq.at[step, t], ret_s.at[step, i], ret_r.at[step, t],
                device_id=dev(k, b), device_id_type=MESH)
            cp.start()
            copies.append(cp)
        rq[step, t] = qs[step, t]
        return copies

    def take_back(step):
        for i in range(1, nt):
            k = lax.rem(t + i, nt)
            pltpu.make_async_remote_copy(
                qs.at[step, k], rq.at[step, k], ret_s.at[step, i], ret_r.at[step, k],
                device_id=dev(k, b), device_id_type=MESH).wait_recv()

        def band(k, carry):
            def put(c, v):
                st[pl.ds((k * cw + c) * rows, rows), :] = v

            unpack_main(lambda j: rq[step, k, j].astype(F32), put)
            return carry

        lax.fori_loop(0, nt, band, 0)

    network(ext)
    sent_1 = give_back(0, 2)

    receive(pb, rb, eb, bar_b_s, bar_b_r, edge_b_r, 1)

    def put_x(s, c, v):
        xb[s, c] = v

    unpack_all(rb, put_x)

    def advance(s, total):
        def one(c, k):
            v = xb[s, c + 2] + 0.5 * score[s + 1, c]
            nu[s + 1, c] = v
            return k

        lax.fori_loop(0, ext - 4, one, 0, unroll=2)

        def sq(c, k):
            v = nu[s + 1, c + 2]
            return k + v * v

        return lax.fori_loop(0, cw, sq, total, unroll=2)

    total = lax.fori_loop(0, nt, advance, jnp.zeros((rows, LANES), F32))
    part = total[0:8]
    for i in range(1, rows // 8):
        part = part + total[8 * i : 8 * i + 8]
    scale = reduced(1, part, False)

    def rescale(s, carry):
        def one(c, k):
            nu[s + 1, c] = (nu[s + 1, c] * scale).astype(BF16).astype(F32)
            return k

        return lax.fori_loop(0, ext - 4, one, carry, unroll=2)

    lax.fori_loop(0, nt, rescale, 0)
    network(ext - 4)
    sent_2 = give_back(1, 0)

    take_back(0)

    def add_first(r, c):
        v = st[pl.ds(r, cols, stride=rows), :].T
        at = pl.ds(r, LANES, stride=rows)
        base[at, :] = base[at, :] + quot[pl.ds(r, 1), :] * v
        return c

    lax.fori_loop(0, rows, add_first, 0)
    take_back(1)

    def add_second(r, c):
        v = st[pl.ds(r, cols, stride=rows), :].T
        at = pl.ds(r, LANES, stride=rows)
        base[at, :] = base[at, :] + 0.5 * v
        return c

    lax.fori_loop(0, rows, add_second, 0)
    out_ref[...] = base[0 : nvar * rows, :]
    for cp in sent_n + sent_b + sent_1 + sent_2:
        cp.wait_send()


def body(states, obs_index, obs_values, first_weight, first_bias, second_weight):
    nt, nl = lax.axis_size("traj"), lax.axis_size("lon")
    _, nvar, rows, cols = states.shape
    hid = first_bias.shape[0]
    band = lax.axis_index("lon")
    lon_total = cols * nl
    loc = obs_index // lon_total * cols + obs_index % lon_total - band * cols
    wide = 2 * LANES
    w1 = first_weight.reshape(hid, 3, 3, 3 * nvar)
    w1 = jnp.pad(w1, ((0, 0), (0, 0), (0, 0), (0, wide - 3 * nvar)))
    w1 = w1.transpose(2, 1, 3, 0).reshape(9 * wide, hid)
    w2 = jnp.pad(second_weight, ((0, wide - 3 * nvar), (0, 0))).reshape(wide, 3, 3, hid)
    w2 = w2.transpose(2, 1, 3, 0).reshape(9 * hid, wide)
    cw = cols // nt
    ext = cw + 4 * STEPS
    mt = 5 * cw // 8
    tiles = mt + 6
    nobs = obs_values.shape[2]
    dma = pltpu.SemaphoreType.DMA
    vm = pltpu.VMEM
    big = LANES * rows
    scratch = [
        vm((big, LANES), F32), vm((cols * rows, LANES), F32), vm((big, LANES), F32), vm((rows, LANES), F32),
        vm((1, LANES, nobs), F32), vm((cols * rows, LANES), F32),
        vm((nt + 2, tiles, rows, LANES), BF16), vm((nt + 2, tiles, rows, LANES), BF16),
        vm((nt, tiles, rows, LANES), BF16), vm((nt, tiles, rows, LANES), BF16),
        vm((nt, 3, rows, LANES), BF16), vm((nt, 3, rows, LANES), BF16),
        vm((nt + 2, ext, rows, LANES), F32), vm((nt, ext, rows, LANES), F32),
        vm((ext, rows, 3 * wide), BF16), vm((ext * rows, wide), F32), vm((ext, rows, 3 * hid), BF16),
        vm((nt + 2, ext - 4, rows, LANES), F32),
        vm((STEPS, nt, mt, rows, LANES), BF16), vm((STEPS, nt, mt, rows, LANES), BF16),
        vm((cols * rows, LANES), F32),
        vm((STEPS, nt, 8, LANES), F32), vm((STEPS, 2, 8, LANES), F32), vm((STEPS, nl, 8, LANES), F32),
        dma((nt,)), dma((nt,)), dma((nt,)), dma((nt,)), dma((2, 2)), dma((nt,)), dma((nt,)),
        dma((STEPS, nt)), dma((STEPS, nt)),
        dma((STEPS, nt)), dma((STEPS, nt)), dma((STEPS, nl)), dma((STEPS, nl)),
    ]
    out = pl.pallas_call(
        functools.partial(kernel, nt, nl, nvar, rows, cols, hid),
        out_shape=jax.ShapeDtypeStruct((nvar * rows, cols), F32),
        in_specs=[pl.BlockSpec(memory_space=vm)] * 6,
        out_specs=pl.BlockSpec(memory_space=vm),
        scratch_shapes=scratch,
        compiler_params=pltpu.CompilerParams(
            collective_id=0, has_side_effects=True, vmem_limit_bytes=60 << 20),
    )(states.reshape(nvar * rows, cols), loc, obs_values[0], w1, first_bias.reshape(1, hid), w2)
    return out.reshape(1, nvar, rows, cols)


def solution(mesh):
    placed = (P("traj", None, None, "lon"), P("traj", "lon"), P("traj", None, "lon"), P(), P(), P())
    return jax.shard_map(
        body, mesh=mesh, in_specs=placed, out_specs=P("traj", None, None, "lon"), check_vma=False
    )
```

```python
import functools

import jax
import jax.numpy as jnp
from jax import lax
from jax.experimental import pallas as pl
from jax.experimental.pallas import tpu as pltpu
from jax.sharding import PartitionSpec as P

STEPS = 2
F32 = jnp.float32
BF16 = jnp.bfloat16
LANES = 128
HALF = 64
PIECE = 16
GROUP = 4
MESH = pl.DeviceIdType.MESH


def lane_of(shape):
    return lax.broadcasted_iota(jnp.int32, shape, len(shape) - 1)


def turned(value, by):
    by = by % LANES
    return value if by == 0 else pltpu.roll(value, by, len(value.shape) - 1)


def pack_pair(low, high):
    return jnp.where(lane_of(low.shape) < HALF, low, turned(high, HALF))


def pack_tails(cols):
    out = jnp.zeros_like(cols[0])
    lane = lane_of(out.shape)
    for i, col in enumerate(cols):
        out = jnp.where(lane // PIECE == i, turned(col, PIECE * i - HALF), out)
    return out


def kernel(
    nt, nl, nvar, rows, cols, hid,
    x_ref, loc_ref, val_ref, w1_ref, b1_ref, w2_ref, out_ref,
    xn, xt, base, quot, obs3, bt, pn, pb, rn, rb, en, eb, nu, xb, x3, acc, h3, score,
    qs, rq, st, red1, sum1, red2,
    bar_n_s, bar_n_r, bar_b_s, bar_b_r, edge_s, edge_n_r, edge_b_r, ret_s, ret_r,
    r1_s, r1_r, r2_s, r2_r, w1p, w2p, w1s, w2s,
):
    t = lax.axis_index("traj")
    b = lax.axis_index("lon")
    cw = cols // nt
    halo = 2 * STEPS
    ext = cw + 2 * halo
    mt = 5 * cw // 8
    tiles = mt + 6
    count = nt * rows * cols * nl
    lane = lane_of((rows, LANES))
    row = lax.broadcasted_iota(jnp.int32, (rows, LANES), 0)

    def dev(tt, bb):
        return {"traj": lax.rem(tt, nt), "lon": lax.rem(bb, nl)}

    barrier = pltpu.get_barrier_semaphore()
    partners = 0
    for db in range(nl):
        for dt in range(nt):
            near = db in (0, 1, nl - 1)
            if (db or dt) and (near or dt == 0):
                pl.semaphore_signal(barrier, inc=1, device_id=dev(t + dt, b + db), device_id_type=MESH)
                partners += 1

    xn[0 : nvar * rows, :] = x_ref[...]
    xn[nvar * rows :, :] = jnp.zeros((LANES * rows - nvar * rows, LANES), F32)

    def flip(r, c):
        xt[pl.ds(r, cols, stride=rows), :] = xn[pl.ds(r, LANES, stride=rows), :].T
        return c

    lax.fori_loop(0, rows, flip, 0)

    def squares(ref, first, n):
        def one(i, c):
            v = ref[pl.ds(first + i * 32, 32), :]
            return c + v * v

        s = lax.fori_loop(0, n // 32, one, jnp.zeros((32, LANES), F32))
        return s[0:8] + s[8:16] + s[16:24] + s[24:32]

    def reduced(step, part, first):
        sum1[step, 0] = part
        copies = []
        for i in range(1, nt):
            cp = pltpu.make_async_remote_copy(
                sum1.at[step, 0], red1.at[step, i], r1_s.at[step, i], r1_r.at[step, i],
                device_id=dev(t + i, b), device_id_type=MESH)
            cp.start()
            copies.append(cp)
        tot = part
        for i in range(1, nt):
            copies[i - 1].wait()
            tot = tot + red1[step, i]
        sum1[step, 1] = tot
        copies = []
        for i in range(1, nl):
            cp = pltpu.make_async_remote_copy(
                sum1.at[step, 1], red2.at[step, i], r2_s.at[step, i], r2_r.at[step, i],
                device_id=dev(t, b + i), device_id_type=MESH)
            cp.start()
            copies.append(cp)
        for i in range(1, nl):
            copies[i - 1].wait()
            tot = tot + red2[step, i]
        moment = jnp.sum(tot, axis=0, keepdims=True) / count
        return 1.0 / jnp.sqrt(moment + 1e-06)

    part = squares(xt, 0, cols * rows)
    pl.semaphore_wait(barrier, partners)
    scale = reduced(0, part, True)

    def tiled(value):
        return value.reshape(-1, rows, LANES)

    def flat(value):
        return value.reshape(-1, LANES)

    def pack_main(get, put):
        step = cw // 8
        for i in range(4):
            put(i * step, pack_pair(get(i * step, step), get(cw // 2 + i * step, step)))
        put(cw // 2, pack_tails([get(step * i, step) for i in range(8)]))

    def pack_all(get, dest):
        zero = jnp.zeros((3, rows, LANES), BF16)
        dest[1, 0:3] = zero
        dest[nt, tiles - 3 :] = zero

        def sub(k, carry):
            def put(j, v):
                dest[k + 1, pl.ds(3 + j, v.shape[0] // rows)] = tiled(v.astype(BF16))

            pack_main(lambda c, n: get(k * cw + c, n), put)
            for first, slot, at in ((k * cw, k, tiles - 3), (k * cw + cw - halo, k + 2, 0)):
                dest[slot, at : at + 2] = tiled(pack_pair(get(first, 2), get(first + 2, 2)).astype(BF16))
                dest[slot, at + 2] = pack_tails([get(first + i, 1) for i in range(4)]).astype(BF16)
            return carry

        lax.fori_loop(0, nt, sub, 0)

    def send_all(src, dst, edge, s_sem, r_sem, e_sem, f):
        copies = []
        for i in range(1, nt):
            k = lax.rem(t + i, nt)
            cp = pltpu.make_async_remote_copy(
                src.at[k + 1], dst.at[t], s_sem.at[i], r_sem.at[t],
                device_id=dev(k, b), device_id_type=MESH)
            cp.start()
            copies.append(cp)
        right = pltpu.make_async_remote_copy(
            src.at[nt + 1, 0:3], edge.at[t], edge_s.at[f, 0], e_sem.at[t],
            device_id=dev(0, b + 1), device_id_type=MESH)
        left = pltpu.make_async_remote_copy(
            src.at[0, tiles - 3 : tiles], edge.at[t], edge_s.at[f, 1], e_sem.at[t],
            device_id=dev(nt - 1, b + nl - 1), device_id_type=MESH)
        right.start()
        left.start()
        dst[t] = src[t + 1]
        return copies + [right, left]

    def receive(src, dst, edge, s_sem, r_sem, e_sem, f):
        for i in range(1, nt):
            k = lax.rem(t + i, nt)
            pltpu.make_async_remote_copy(
                src.at[k + 1], dst.at[k], s_sem.at[i], r_sem.at[k],
                device_id=dev(k, b), device_id_type=MESH).wait_recv()

        def edges(at, side):
            for k in range(nt):
                pltpu.make_async_remote_copy(
                    src.at[0, 0:3], edge.at[k], edge_s.at[f, 0], e_sem.at[k],
                    device_id=dev(0, b + 1), device_id_type=MESH).wait_recv()
                dst[k, at : at + 3] = edge[k]

        @pl.when(t == 0)
        def _():
            edges(0, 1)

        @pl.when(t == nt - 1)
        def _():
            edges(tiles - 3, -1)

    def unpack_main(tile, put):
        step = cw // 8
        tail = tile(cw // 2, step)
        for i in range(8):
            a = turned(tile((i % 4) * step, step), HALF * (i // 4))
            put(i * step, jnp.where(lane_of(a.shape) < HALF, a, turned(tail, HALF - PIECE * i)))

    def unpack_all(src, put):
        def state(s, carry):
            def tile(j, n):
                return flat(src[s, pl.ds(j, n)].astype(F32))

            for at, first in ((0, 0), (tiles - 3, cw + halo)):
                pairs = tile(at, 2)
                tail = tile(at + 2, 1)
                for i in range(4):
                    a = turned(pairs[(i % 2) * rows : (i % 2 + 1) * rows], HALF * (i // 2))
                    put(s, first + i, jnp.where(lane < HALF, a, turned(tail, HALF - PIECE * i)))
            unpack_main(lambda j, n: tile(3 + j, n), lambda c, v: put(s, c + halo, v))
            return carry

        lax.fori_loop(0, nt, state, 0)

    pack_all(lambda c, n: xt[pl.ds(c * rows, n * rows), :] * scale, pn)
    sent_n = send_all(pn, rn, en, bar_n_s, bar_n_r, edge_n_r, 0)

    vals = jnp.concatenate([val_ref[...], jnp.ones((8, val_ref.shape[1]), F32)], 0) if nvar % 8 == 0 else None
    if vals is None:
        obs_rows = val_ref.shape[0]
        obs3[0, 0:obs_rows] = val_ref[...]
        obs3[0, obs_rows:] = jnp.ones((LANES - obs_rows, val_ref.shape[1]), F32)
    else:
        obs3[0, 0 : nvar + 8] = vals
        obs3[0, nvar + 8 :] = jnp.zeros((LANES - nvar - 8, val_ref.shape[1]), F32)
    full = obs3[0]
    high = full.astype(BF16)
    rest = full - high.astype(F32)
    mid = rest.astype(BF16)
    low = (rest - mid.astype(F32)).astype(BF16)
    three = jnp.concatenate([high, mid, low], 0)
    loc = loc_ref[...]

    def observe(r, c):
        cell = lax.broadcasted_iota(jnp.int32, (cols, loc.shape[1]), 0) + r * cols
        hot = jnp.where(cell == loc, 1.0, 0.0).astype(BF16)
        o = lax.dot_general(three, hot, (((1,), (1,)), ((), ())), preferred_element_type=F32)
        o = o[0:LANES] + o[LANES : 2 * LANES] + o[2 * LANES :]
        seen = o[nvar : nvar + 1, :] > 0.5
        x = xn[pl.ds(r, LANES, stride=rows), :]
        g = jnp.where(seen, 0.5 * (o - x), 0.0)
        base[pl.ds(r, LANES, stride=rows), :] = jnp.where(seen, 0.5 * (x + g + o), x)
        quot[pl.ds(r, 1), :] = jnp.where(seen, 0.25, 0.5)
        bt[pl.ds(r, cols, stride=rows), :] = (x + g).T
        return c

    lax.fori_loop(0, rows, observe, 0)
    pack_all(lambda c, n: bt[pl.ds(c * rows, n * rows), :], pb)
    sent_b = send_all(pb, rb, eb, bar_b_s, bar_b_r, edge_b_r, 1)

    wide = 2 * LANES
    deep = 3 * nvar
    used = w1_ref.shape[1]
    w1p[:, used // LANES * LANES :] = jnp.zeros((hid, w1p.shape[1] - used // LANES * LANES), BF16)
    w1p[:, 0:used] = w1_ref[...]
    w2p[deep // PIECE * PIECE :, :] = jnp.zeros((wide - deep // PIECE * PIECE, w2p.shape[1]), BF16)
    w2p[0:deep, :] = w2_ref[...]
    for a in range(3):
        for k in range(3):
            tap, to = 3 * a + k, 3 * k + a
            at = tap * deep // LANES * LANES
            v = w1p[:, at : at + 3 * LANES].astype(F32)
            off = tap * deep - at
            v = v if off == 0 else pltpu.roll(v, 3 * LANES - off, 1)
            v = jnp.where(lane_of((hid, wide)) < deep, v[:, 0:wide], 0.0)
            w1s[to * wide : (to + 1) * wide, :] = v.T.astype(BF16)
            v = w2p[:, tap * hid : (tap + 1) * hid].astype(F32)
            w2s[to * hid : (to + 1) * hid, :] = v.T.astype(BF16)

    nu[0] = jnp.zeros(nu.shape[1:], F32)
    nu[nt + 1] = jnp.zeros(nu.shape[1:], F32)
    receive(pn, rn, en, bar_n_s, bar_n_r, edge_n_r, 0)

    def put_n(s, c, v):
        nu[s + 1, pl.ds(c, v.shape[0] // rows)] = tiled(v)

    unpack_all(rn, put_n)

    def spread(dest, c, tile_list):
        n = len(tile_list)
        many = tile_list[0].shape[0]
        rown = lax.broadcasted_iota(jnp.int32, (many, LANES), 0) % rows
        for i, v in enumerate(tile_list):
            up = jnp.where(rown == 0, 0.0, pltpu.roll(v, 1, 0))
            down = jnp.where(rown == rows - 1, 0.0, pltpu.roll(v, many - 1, 0))
            for a, piece in enumerate((up, v, down)):
                dest[pl.ds(c, many // rows), :, a * n * LANES + i * LANES : a * n * LANES + (i + 1) * LANES] = tiled(
                    piece.astype(BF16))

    two = 2 * nvar - LANES

    def network(width):
        score[...] = jnp.zeros(score.shape, F32)

        def state(s, carry):
            def window(j, k):
                c = j * GROUP
                before, here, after = [flat(nu[s + i, pl.ds(c, GROUP)]) for i in range(3)]
                lane = lane_of(here.shape)
                moved = turned(here, nvar)
                first = jnp.where(lane < nvar, before, moved)
                last = jnp.where(lane < two, moved, jnp.where(lane < two + nvar, turned(after, two), 0.0))
                spread(x3, c, [first, last])
                return k

            lax.fori_loop(0, width // GROUP, window, 0, unroll=2)
            wid = width - 2
            lhs = jnp.concatenate(
                [x3[i : i + wid].reshape(wid * rows, 3 * wide) for i in range(3)], 1)
            acc[0 : wid * rows, :] = jnp.dot(lhs, w1s[...], preferred_element_type=F32)
            bias = b1_ref[...]

            def activate(j, k):
                c = jnp.minimum(j * GROUP, wid - GROUP)
                v = acc[pl.ds(c * rows, GROUP * rows), :] + bias
                v = v / (1.0 + jnp.exp(-v))
                v = v.astype(BF16).astype(F32)
                spread(h3, c, [v[:, i * LANES : (i + 1) * LANES] for i in range(hid // LANES)])
                return k

            lax.fori_loop(0, -(-wid // GROUP), activate, 0, unroll=2)
            wid = width - 4
            lhs = jnp.concatenate(
                [h3[i : i + wid].reshape(wid * rows, 3 * hid) for i in range(3)], 1)
            acc[0 : wid * rows, :] = jnp.dot(lhs, w2s[...], preferred_element_type=F32)

            def share(j, k):
                c = j * GROUP
                c0 = acc[pl.ds(c * rows, GROUP * rows), 0:LANES]
                c1 = acc[pl.ds(c * rows, GROUP * rows), LANES : 2 * LANES]
                lane = lane_of(c0.shape)
                mid_part = jnp.where(lane < LANES - nvar, turned(c0, -nvar), turned(c1, -nvar))
                at = pl.ds(c, GROUP)
                olds = [score[s + i, at] for i in range(3)]
                news = [old + tiled(v) for old, v in zip(olds, (c0, mid_part, turned(c1, -two)))]
                for i in range(3):
                    score[s + i, at] = news[i]
                return k

            lax.fori_loop(0, wid // GROUP, share, 0)
            return carry

        lax.fori_loop(0, nt, state, 0)

    def give_back(step, off):
        def state(s, carry):
            def get(c, n):
                return flat(score[s + 1, pl.ds(c + off, n)])

            def put(j, v):
                qs[step, s, pl.ds(j, v.shape[0] // rows)] = tiled(v.astype(BF16))

            pack_main(get, put)
            return carry

        lax.fori_loop(0, nt, state, 0)
        copies = []
        for i in range(1, nt):
            k = lax.rem(t + i, nt)
            cp = pltpu.make_async_remote_copy(
                qs.at[step, k], rq.at[step, t], ret_s.at[step, i], ret_r.at[step, t],
                device_id=dev(k, b), device_id_type=MESH)
            cp.start()
            copies.append(cp)
        rq[step, t] = qs[step, t]
        return copies

    def take_back(step):
        for i in range(1, nt):
            k = lax.rem(t + i, nt)
            pltpu.make_async_remote_copy(
                qs.at[step, k], rq.at[step, k], ret_s.at[step, i], ret_r.at[step, k],
                device_id=dev(k, b), device_id_type=MESH).wait_recv()

        def band(k, carry):
            def put(c, v):
                st[pl.ds((k * cw + c) * rows, v.shape[0]), :] = v

            unpack_main(lambda j, n: flat(rq[step, k, pl.ds(j, n)].astype(F32)), put)
            return carry

        lax.fori_loop(0, nt, band, 0)

    network(ext)
    sent_1 = give_back(0, 2)

    receive(pb, rb, eb, bar_b_s, bar_b_r, edge_b_r, 1)

    def put_x(s, c, v):
        xb[s, pl.ds(c, v.shape[0] // rows)] = tiled(v)

    unpack_all(rb, put_x)

    def advance(s, total):
        def one(j, k):
            at = pl.ds(j * GROUP, GROUP)
            nu[s + 1, at] = xb[s, pl.ds(j * GROUP + 2, GROUP)] + 0.5 * score[s + 1, at]
            return k

        lax.fori_loop(0, (ext - 4) // GROUP, one, 0)

        def sq(c, k):
            v = nu[s + 1, c + 2]
            return k + v * v

        return lax.fori_loop(0, cw, sq, total, unroll=2)

    total = lax.fori_loop(0, nt, advance, jnp.zeros((rows, LANES), F32))
    part = total[0:8]
    for i in range(1, rows // 8):
        part = part + total[8 * i : 8 * i + 8]
    scale = reduced(1, part, False)

    def rescale(s, carry):
        def one(j, k):
            at = pl.ds(j * GROUP, GROUP)
            nu[s + 1, at] = (nu[s + 1, at] * scale).astype(BF16).astype(F32)
            return k

        return lax.fori_loop(0, (ext - 4) // GROUP, one, carry)

    lax.fori_loop(0, nt, rescale, 0)
    network(ext - 4)
    sent_2 = give_back(1, 0)

    take_back(0)

    def add_first(r, c):
        v = st[pl.ds(r, cols, stride=rows), :].T
        at = pl.ds(r, LANES, stride=rows)
        base[at, :] = base[at, :] + quot[pl.ds(r, 1), :] * v
        return c

    lax.fori_loop(0, rows, add_first, 0)
    take_back(1)

    def add_second(r, c):
        v = st[pl.ds(r, cols, stride=rows), :].T
        at = pl.ds(r, LANES, stride=rows)
        base[at, :] = base[at, :] + 0.5 * v
        return c

    lax.fori_loop(0, rows, add_second, 0)
    out_ref[...] = base[0 : nvar * rows, :]
    for cp in sent_n + sent_b + sent_1 + sent_2:
        cp.wait_send()


def body(states, obs_index, obs_values, first_weight, first_bias, second_weight):
    nt, nl = lax.axis_size("traj"), lax.axis_size("lon")
    _, nvar, rows, cols = states.shape
    hid = first_bias.shape[0]
    band = lax.axis_index("lon")
    lon_total = cols * nl
    loc = obs_index // lon_total * cols + obs_index % lon_total - band * cols
    wide = 2 * LANES
    span = (9 * 3 * nvar // LANES + 3) * LANES
    cw = cols // nt
    ext = cw + 4 * STEPS
    mt = 5 * cw // 8
    tiles = mt + 6
    nobs = obs_values.shape[2]
    wide = 2 * LANES
    dma = pltpu.SemaphoreType.DMA
    vm = pltpu.VMEM
    big = LANES * rows
    scratch = [
        vm((big, LANES), F32), vm((cols * rows, LANES), F32), vm((big, LANES), F32), vm((rows, LANES), F32),
        vm((1, LANES, nobs), F32), vm((cols * rows, LANES), F32),
        vm((nt + 2, tiles, rows, LANES), BF16), vm((nt + 2, tiles, rows, LANES), BF16),
        vm((nt, tiles, rows, LANES), BF16), vm((nt, tiles, rows, LANES), BF16),
        vm((nt, 3, rows, LANES), BF16), vm((nt, 3, rows, LANES), BF16),
        vm((nt + 2, ext, rows, LANES), F32), vm((nt, ext, rows, LANES), F32),
        vm((ext, rows, 3 * wide), BF16), vm((ext * rows, wide), F32), vm((ext, rows, 3 * hid), BF16),
        vm((nt + 2, ext - 4, rows, LANES), F32),
        vm((STEPS, nt, mt, rows, LANES), BF16), vm((STEPS, nt, mt, rows, LANES), BF16),
        vm((cols * rows, LANES), F32),
        vm((STEPS, nt, 8, LANES), F32), vm((STEPS, 2, 8, LANES), F32), vm((STEPS, nl, 8, LANES), F32),
        dma((nt,)), dma((nt,)), dma((nt,)), dma((nt,)), dma((2, 2)), dma((nt,)), dma((nt,)),
        dma((STEPS, nt)), dma((STEPS, nt)),
        dma((STEPS, nt)), dma((STEPS, nt)), dma((STEPS, nl)), dma((STEPS, nl)),
        vm((hid, span), BF16), vm((wide, 9 * hid), BF16), vm((9 * wide, hid), BF16), vm((9 * hid, wide), BF16),
    ]
    out = pl.pallas_call(
        functools.partial(kernel, nt, nl, nvar, rows, cols, hid),
        out_shape=jax.ShapeDtypeStruct((nvar * rows, cols), F32),
        in_specs=[pl.BlockSpec(memory_space=vm)] * 6,
        out_specs=pl.BlockSpec(memory_space=vm),
        scratch_shapes=scratch,
        compiler_params=pltpu.CompilerParams(
            collective_id=0, has_side_effects=True, vmem_limit_bytes=60 << 20),
    )(states.reshape(nvar * rows, cols), loc, obs_values[0], first_weight, first_bias.reshape(1, hid), second_weight)
    return out.reshape(1, nvar, rows, cols)


def solution(mesh):
    placed = (P("traj", None, None, "lon"), P("traj", "lon"), P("traj", None, "lon"), P(), P(), P())
    return jax.shard_map(
        body, mesh=mesh, in_specs=placed, out_specs=P("traj", None, None, "lon"), check_vma=False
    )
```

```python
import functools

import jax
import jax.numpy as jnp
from jax import lax
from jax.experimental import pallas as pl
from jax.experimental.pallas import tpu as pltpu
from jax.sharding import PartitionSpec as P

STEPS = 2
F32 = jnp.float32
BF16 = jnp.bfloat16
LANES = 128
HALF = 64
PIECE = 16
GROUP = 4
MESH = pl.DeviceIdType.MESH


def lane_of(shape):
    return lax.broadcasted_iota(jnp.int32, shape, len(shape) - 1)


def turned(value, by):
    by = by % LANES
    return value if by == 0 else pltpu.roll(value, by, len(value.shape) - 1)


def pack_pair(low, high):
    return jnp.where(lane_of(low.shape) < HALF, low, turned(high, HALF))


def pack_tails(cols):
    out = jnp.zeros_like(cols[0])
    lane = lane_of(out.shape)
    for i, col in enumerate(cols):
        out = jnp.where(lane // PIECE == i, turned(col, PIECE * i - HALF), out)
    return out


def kernel(
    nt, nl, nvar, rows, cols, hid,
    x_ref, loc_ref, val_ref, w1_ref, b1_ref, w2_ref, out_ref,
    xn, xt, base, quot, obs3, bt, pn, pb, rn, rb, en, eb, nu, xb, x3, acc, h3, score,
    qs, rq, st, red1, sum1, red2,
    bar_n_s, bar_n_r, bar_b_s, bar_b_r, edge_s, edge_n_r, edge_b_r, ret_s, ret_r,
    r1_s, r1_r, r2_s, r2_r, w2p, w1s, w2s,
):
    t = lax.axis_index("traj")
    b = lax.axis_index("lon")
    cw = cols // nt
    halo = 2 * STEPS
    ext = cw + 2 * halo
    mt = 5 * cw // 8
    tiles = mt + 6
    count = nt * rows * cols * nl
    lane = lane_of((rows, LANES))
    row = lax.broadcasted_iota(jnp.int32, (rows, LANES), 0)

    def dev(tt, bb):
        return {"traj": lax.rem(tt, nt), "lon": lax.rem(bb, nl)}

    upward = 2 * t < nt

    def nth(i):
        return jnp.where(upward, i, nt - 1 - i)

    own_place = nth(t)

    def other(j):
        return nth(j + jnp.where(j >= own_place, 1, 0))

    barrier = pltpu.get_barrier_semaphore()
    partners = 0
    for db in range(nl):
        for dt in range(nt):
            near = db in (0, 1, nl - 1)
            if (db or dt) and (near or dt == 0):
                pl.semaphore_signal(barrier, inc=1, device_id=dev(t + dt, b + db), device_id_type=MESH)
                partners += 1

    xn[0 : nvar * rows, :] = x_ref[...]
    xn[nvar * rows :, :] = jnp.zeros((LANES * rows - nvar * rows, LANES), F32)

    def flip(r, c):
        xt[pl.ds(r, cols, stride=rows), :] = xn[pl.ds(r, LANES, stride=rows), :].T
        return c

    lax.fori_loop(0, rows, flip, 0, unroll=4)

    def squares(ref, first, n):
        def one(i, c):
            v = ref[pl.ds(first + i * 32, 32), :]
            return c + v * v

        s = lax.fori_loop(0, n // 32, one, jnp.zeros((32, LANES), F32))
        return s[0:8] + s[8:16] + s[16:24] + s[24:32]

    def sum_over_traj(step, part):
        sum1[step, 0] = part
        copies = [
            pltpu.make_async_remote_copy(
                sum1.at[step, 0], red1.at[step, i], r1_s.at[step, i], r1_r.at[step, i],
                device_id=dev(t + i, b), device_id_type=MESH)
            for i in range(1, nt)]
        for cp in copies:
            cp.start()
        return copies

    def sum_over_lon(step, part, copies):
        tot = part
        for i, cp in enumerate(copies):
            cp.wait()
            tot = tot + red1[step, i + 1]
        sum1[step, 1] = tot
        copies = [
            pltpu.make_async_remote_copy(
                sum1.at[step, 1], red2.at[step, i], r2_s.at[step, i], r2_r.at[step, i],
                device_id=dev(t, b + i), device_id_type=MESH)
            for i in range(1, nl)]
        for cp in copies:
            cp.start()
        return tot, copies

    def scale_of(step, tot, copies):
        for i, cp in enumerate(copies):
            cp.wait()
            tot = tot + red2[step, i + 1]
        moment = jnp.sum(tot, axis=0, keepdims=True) / count
        return 1.0 / jnp.sqrt(moment + 1e-06)

    part = squares(xt, 0, cols * rows)
    pl.semaphore_wait(barrier, partners)
    moving = sum_over_traj(0, part)

    obs3[0] = jnp.ones(obs3.shape[1:], F32)
    obs3[0, 0:nvar] = val_ref[:, 0, :]
    full = obs3[0]
    high = full.astype(BF16)
    rest = full - high.astype(F32)
    mid = rest.astype(BF16)
    low = (rest - mid.astype(F32)).astype(BF16)
    three = jnp.concatenate([high, mid, low], 0)
    loc = loc_ref[...]

    def observe(r, c):
        cell = lax.broadcasted_iota(jnp.int32, (cols, loc.shape[1]), 0) + (r * cols * nl + b * cols)
        hot = jnp.where(cell == loc, 1.0, 0.0).astype(BF16)
        o = lax.dot_general(three, hot, (((1,), (1,)), ((), ())), preferred_element_type=F32)
        o = o[0:LANES] + o[LANES : 2 * LANES] + o[2 * LANES :]
        seen = o[nvar : nvar + 1, :] > 0.5
        x = xn[pl.ds(r, LANES, stride=rows), :]
        g = jnp.where(seen, 0.5 * (o - x), 0.0)
        base[pl.ds(r, LANES, stride=rows), :] = jnp.where(seen, 0.5 * (x + g + o), x)
        quot[pl.ds(r, 1), :] = jnp.where(seen, 0.25, 0.5)
        bt[pl.ds(r, cols, stride=rows), :] = (x + g).T
        return c

    lax.fori_loop(0, rows, observe, 0, unroll=2)
    part, moving = sum_over_lon(0, part, moving)

    wide = 2 * LANES
    deep = 3 * nvar
    w2p[deep // PIECE * PIECE :, :] = jnp.zeros((wide - deep // PIECE * PIECE, w2p.shape[1]), BF16)
    w2p[0:deep, :] = w2_ref[...]
    for a in range(3):
        for k in range(3):
            tap, to = 3 * a + k, 3 * k + a
            w1s[(to + 1) * wide - 2 * PIECE : (to + 1) * wide, :] = jnp.zeros((2 * PIECE, hid), BF16)
            w1s[to * wide : to * wide + deep, :] = w1_ref[tap * deep : (tap + 1) * deep, :]
            v = w2p[:, tap * hid : (tap + 1) * hid].astype(F32)
            w2s[to * hid : (to + 1) * hid, :] = v.T.astype(BF16)

    scale = scale_of(0, part, moving)

    def tiled(value):
        return value.reshape(-1, rows, LANES)

    def flat(value):
        return value.reshape(-1, LANES)

    def pack_main(get, put):
        step = cw // 8
        for i in range(4):
            put(i * step, pack_pair(get(i * step, step), get(cw // 2 + i * step, step)))
        put(cw // 2, pack_tails([get(step * i, step) for i in range(8)]))

    def pack_all(get, dest):
        zero = jnp.zeros((3, rows, LANES), BF16)
        dest[1, 0:3] = zero
        dest[nt, tiles - 3 :] = zero

        def sub(k, carry):
            def put(j, v):
                dest[k + 1, pl.ds(3 + j, v.shape[0] // rows)] = tiled(v.astype(BF16))

            pack_main(lambda c, n: get(k * cw + c, n), put)
            for first, slot, at in ((k * cw, k, tiles - 3), (k * cw + cw - halo, k + 2, 0)):
                dest[slot, at : at + 2] = tiled(pack_pair(get(first, 2), get(first + 2, 2)).astype(BF16))
                dest[slot, at + 2] = pack_tails([get(first + i, 1) for i in range(4)]).astype(BF16)
            return carry

        lax.fori_loop(0, nt, sub, 0)

    def send_all(src, dst, edge, s_sem, r_sem, e_sem, f):
        right = pltpu.make_async_remote_copy(
            src.at[nt + 1, 0:3], edge.at[t], edge_s.at[f, 0], e_sem.at[t],
            device_id=dev(0, b + 1), device_id_type=MESH)
        left = pltpu.make_async_remote_copy(
            src.at[0, tiles - 3 : tiles], edge.at[t], edge_s.at[f, 1], e_sem.at[t],
            device_id=dev(nt - 1, b + nl - 1), device_id_type=MESH)
        right.start()
        left.start()
        copies = [right, left]
        for j in range(nt - 1):
            k = other(j)
            cp = pltpu.make_async_remote_copy(
                src.at[k + 1], dst.at[t], s_sem.at[j], r_sem.at[t],
                device_id=dev(k, b), device_id_type=MESH)
            cp.start()
            copies.append(cp)
        dst[t] = src[t + 1]
        return copies

    def receive(s, src, dst, edge, s_sem, r_sem, e_sem, f):
        @pl.when(s != t)
        def _():
            pltpu.make_async_remote_copy(
                src.at[s + 1], dst.at[s], s_sem.at[0], r_sem.at[s],
                device_id=dev(s, b), device_id_type=MESH).wait_recv()

        def edges(at):
            pltpu.make_async_remote_copy(
                src.at[0, 0:3], edge.at[s], edge_s.at[f, 0], e_sem.at[s],
                device_id=dev(0, b + 1), device_id_type=MESH).wait_recv()
            dst[s, at : at + 3] = edge[s]

        @pl.when(t == 0)
        def _():
            edges(0)

        @pl.when(t == nt - 1)
        def _():
            edges(tiles - 3)

    def unpack_main(tile, put):
        step = cw // 8
        tail = tile(cw // 2, step)
        for i in range(8):
            a = turned(tile((i % 4) * step, step), HALF * (i // 4))
            put(i * step, jnp.where(lane_of(a.shape) < HALF, a, turned(tail, HALF - PIECE * i)))

    def unpack_state(s, src, put):
        def tile(j, n):
            return flat(src[s, pl.ds(j, n)].astype(F32))

        for at, first in ((0, 0), (tiles - 3, cw + halo)):
            pairs = tile(at, 2)
            tail = tile(at + 2, 1)
            for i in range(4):
                a = turned(pairs[(i % 2) * rows : (i % 2 + 1) * rows], HALF * (i // 2))
                put(s, first + i, jnp.where(lane < HALF, a, turned(tail, HALF - PIECE * i)))
        unpack_main(lambda j, n: tile(3 + j, n), lambda c, v: put(s, c + halo, v))

    pack_all(lambda c, n: xt[pl.ds(c * rows, n * rows), :] * scale, pn)
    sent_n = send_all(pn, rn, en, bar_n_s, bar_n_r, edge_n_r, 0)

    pack_all(lambda c, n: bt[pl.ds(c * rows, n * rows), :], pb)
    sent_b = send_all(pb, rb, eb, bar_b_s, bar_b_r, edge_b_r, 1)

    nu[0] = jnp.zeros(nu.shape[1:], F32)
    nu[nt + 1] = jnp.zeros(nu.shape[1:], F32)

    def put_n(s, c, v):
        nu[s + 1, pl.ds(c, v.shape[0] // rows)] = tiled(v)

    def arrive(s):
        receive(s, pn, rn, en, bar_n_s, bar_n_r, edge_n_r, 0)
        unpack_state(s, rn, put_n)

    def spread(dest, c, tile_list):
        n = len(tile_list)
        many = tile_list[0].shape[0]
        rown = lax.broadcasted_iota(jnp.int32, (many, LANES), 0) % rows
        for i, v in enumerate(tile_list):
            up = jnp.where(rown == 0, 0.0, pltpu.roll(v, 1, 0))
            down = jnp.where(rown == rows - 1, 0.0, pltpu.roll(v, many - 1, 0))
            for a, piece in enumerate((up, v, down)):
                dest[pl.ds(c, many // rows), :, a * n * LANES + i * LANES : a * n * LANES + (i + 1) * LANES] = tiled(
                    piece.astype(BF16))

    two = 2 * nvar - LANES

    def give_back(s, step, off):
        def get(c, n):
            return flat(score[s + 1, pl.ds(c + off, n)])

        def put(j, v):
            qs[step, s, pl.ds(j, v.shape[0] // rows)] = tiled(v.astype(BF16))

        pack_main(get, put)

        @pl.when(s != t)
        def _():
            pltpu.make_async_remote_copy(
                qs.at[step, s], rq.at[step, t], ret_s.at[step, s], ret_r.at[step, t],
                device_id=dev(s, b), device_id_type=MESH).start()

        @pl.when(s == t)
        def _():
            rq[step, t] = qs[step, s]

    def network(width, step, off):
        score[...] = jnp.zeros(score.shape, F32)

        def state(i, carry):
            s = nth(i) if step == 0 else nth(nt - 1 - i)
            if step == 0:
                @pl.when(i < nt - 1)
                def _():
                    arrive(nth(i + 1))

            def window(j, k):
                c = j * GROUP
                before, here, after = [flat(nu[s + i, pl.ds(c, GROUP)]) for i in range(3)]
                lane = lane_of(here.shape)
                moved = turned(here, nvar)
                first = jnp.where(lane < nvar, before, moved)
                last = jnp.where(lane < two, moved, jnp.where(lane < two + nvar, turned(after, two), 0.0))
                spread(x3, c, [first, last])
                return k

            lax.fori_loop(0, width // GROUP, window, 0, unroll=2)
            wid = width - 2
            lhs = jnp.concatenate(
                [x3[i : i + wid].reshape(wid * rows, 3 * wide) for i in range(3)], 1)
            acc[0 : wid * rows, :] = jnp.dot(lhs, w1s[...], preferred_element_type=F32)
            bias = b1_ref[...]

            def activate(j, k):
                c = jnp.minimum(j * GROUP, wid - GROUP)
                v = acc[pl.ds(c * rows, GROUP * rows), :] + bias
                v = 0.5 * v
                v = v + v * jnp.tanh(v)
                v = v.astype(BF16).astype(F32)
                spread(h3, c, [v[:, i * LANES : (i + 1) * LANES] for i in range(hid // LANES)])
                return k

            lax.fori_loop(0, -(-wid // GROUP), activate, 0, unroll=2)
            wid = width - 4
            lhs = jnp.concatenate(
                [h3[i : i + wid].reshape(wid * rows, 3 * hid) for i in range(3)], 1)
            acc[0 : wid * rows, :] = jnp.dot(lhs, w2s[...], preferred_element_type=F32)

            def share(j, k):
                c = j * GROUP
                c0 = acc[pl.ds(c * rows, GROUP * rows), 0:LANES]
                c1 = acc[pl.ds(c * rows, GROUP * rows), LANES : 2 * LANES]
                lane = lane_of(c0.shape)
                mid_part = jnp.where(lane < LANES - nvar, turned(c0, -nvar), turned(c1, -nvar))
                at = pl.ds(c, GROUP)
                olds = [score[s + i, at] for i in range(3)]
                news = [old + tiled(v) for old, v in zip(olds, (c0, mid_part, turned(c1, -two)))]
                for i in range(3):
                    score[s + i, at] = news[i]
                return k

            lax.fori_loop(0, wid // GROUP, share, 0)

            @pl.when(i > 0)
            def _():
                give_back(nth(i - 1) if step == 0 else nth(nt - i), step, off)

            return carry

        lax.fori_loop(0, nt, state, 0)
        give_back(nth(nt - 1) if step == 0 else nth(0), step, off)

    def take_back(step):
        for i in range(1, nt):
            k = lax.rem(t + i, nt)
            pltpu.make_async_remote_copy(
                qs.at[step, k], rq.at[step, k], ret_s.at[step, k], ret_r.at[step, k],
                device_id=dev(k, b), device_id_type=MESH).wait_recv()

        def band(k, carry):
            def put(c, v):
                st[pl.ds((k * cw + c) * rows, v.shape[0]), :] = v

            unpack_main(lambda j, n: flat(rq[step, k, pl.ds(j, n)].astype(F32)), put)
            return carry

        lax.fori_loop(0, nt, band, 0)

    arrive(nth(0))
    network(ext, 0, 2)


    def put_x(s, c, v):
        xb[s, pl.ds(c, v.shape[0] // rows)] = tiled(v)

    def arrive_base(i, carry):
        s = nth(i)
        receive(s, pb, rb, eb, bar_b_s, bar_b_r, edge_b_r, 1)
        unpack_state(s, rb, put_x)
        return carry

    lax.fori_loop(0, nt, arrive_base, 0)

    def advance(s, total):
        def one(j, k):
            at = pl.ds(j * GROUP, GROUP)
            nu[s + 1, at] = xb[s, pl.ds(j * GROUP + 2, GROUP)] + 0.5 * score[s + 1, at]
            return k

        lax.fori_loop(0, (ext - 4) // GROUP, one, 0)

        def sq(c, k):
            v = nu[s + 1, c + 2]
            return k + v * v

        return lax.fori_loop(0, cw, sq, total, unroll=2)

    total = lax.fori_loop(0, nt, advance, jnp.zeros((rows, LANES), F32))
    part = total[0:8]
    for i in range(1, rows // 8):
        part = part + total[8 * i : 8 * i + 8]
    moving = sum_over_traj(1, part)
    part, moving = sum_over_lon(1, part, moving)
    scale = scale_of(1, part, moving)

    def rescale(s, carry):
        def one(j, k):
            at = pl.ds(j * GROUP, GROUP)
            nu[s + 1, at] = (nu[s + 1, at] * scale).astype(BF16).astype(F32)
            return k

        return lax.fori_loop(0, (ext - 4) // GROUP, one, carry)

    lax.fori_loop(0, nt, rescale, 0)
    network(ext - 4, 1, 0)

    take_back(0)

    def add_first(r, c):
        v = st[pl.ds(r, cols, stride=rows), :].T
        at = pl.ds(r, LANES, stride=rows)
        base[at, :] = base[at, :] + quot[pl.ds(r, 1), :] * v
        return c

    lax.fori_loop(0, rows, add_first, 0)
    take_back(1)

    def add_second(r, c):
        v = st[pl.ds(r, cols, stride=rows), :].T
        at = pl.ds(r, LANES, stride=rows)
        base[at, :] = base[at, :] + 0.5 * v
        return c

    lax.fori_loop(0, rows, add_second, 0)
    out_ref[...] = base[0 : nvar * rows, :]
    for cp in sent_n + sent_b:
        cp.wait_send()
    for step in range(STEPS):
        for i in range(1, nt):
            k = lax.rem(t + i, nt)
            pltpu.make_async_remote_copy(
                qs.at[step, k], rq.at[step, t], ret_s.at[step, k], ret_r.at[step, t],
                device_id=dev(k, b), device_id_type=MESH).wait_send()


def body(states, obs_index, obs_values, first_weight, first_bias, second_weight):
    nt, nl = lax.axis_size("traj"), lax.axis_size("lon")
    _, nvar, rows, cols = states.shape
    hid = first_bias.shape[0]
    wide = 2 * LANES
    cw = cols // nt
    ext = cw + 4 * STEPS
    mt = 5 * cw // 8
    tiles = mt + 6
    nobs = obs_values.shape[2]
    dma = pltpu.SemaphoreType.DMA
    vm = pltpu.VMEM
    big = LANES * rows
    scratch = [
        vm((big, LANES), F32), vm((cols * rows, LANES), F32), vm((big, LANES), F32), vm((rows, LANES), F32),
        vm((1, LANES, nobs), F32), vm((cols * rows, LANES), F32),
        vm((nt + 2, tiles, rows, LANES), BF16), vm((nt + 2, tiles, rows, LANES), BF16),
        vm((nt, tiles, rows, LANES), BF16), vm((nt, tiles, rows, LANES), BF16),
        vm((nt, 3, rows, LANES), BF16), vm((nt, 3, rows, LANES), BF16),
        vm((nt + 2, ext, rows, LANES), F32), vm((nt, ext, rows, LANES), F32),
        vm((ext, rows, 3 * wide), BF16), vm((ext * rows, wide), F32), vm((ext, rows, 3 * hid), BF16),
        vm((nt + 2, ext - 4, rows, LANES), F32),
        vm((STEPS, nt, mt, rows, LANES), BF16), vm((STEPS, nt, mt, rows, LANES), BF16),
        vm((cols * rows, LANES), F32),
        vm((STEPS, nt, 8, LANES), F32), vm((STEPS, 2, 8, LANES), F32), vm((STEPS, nl, 8, LANES), F32),
        dma((nt,)), dma((nt,)), dma((nt,)), dma((nt,)), dma((2, 2)), dma((nt,)), dma((nt,)),
        dma((STEPS, nt)), dma((STEPS, nt)),
        dma((STEPS, nt)), dma((STEPS, nt)), dma((STEPS, nl)), dma((STEPS, nl)),
        vm((wide, 9 * hid), BF16), vm((9 * wide, hid), BF16), vm((9 * hid, wide), BF16),
    ]
    out = pl.pallas_call(
        functools.partial(kernel, nt, nl, nvar, rows, cols, hid),
        out_shape=jax.ShapeDtypeStruct((nvar * rows, cols), F32),
        in_specs=[pl.BlockSpec(memory_space=vm)] * 6,
        out_specs=pl.BlockSpec(memory_space=vm),
        scratch_shapes=scratch,
        compiler_params=pltpu.CompilerParams(
            collective_id=0, has_side_effects=True, vmem_limit_bytes=60 << 20),
    )(states.reshape(nvar * rows, cols), obs_index, obs_values.reshape(nvar, 1, nobs), first_weight.T, first_bias.reshape(1, hid), second_weight)
    return out.reshape(1, nvar, rows, cols)


def solution(mesh):
    placed = (P("traj", None, None, "lon"), P("traj", "lon"), P("traj", None, "lon"), P(), P(), P())
    return jax.shard_map(
        body, mesh=mesh, in_specs=placed, out_specs=P("traj", None, None, "lon"), check_vma=False
    )
```

```python
import functools

import jax
import jax.numpy as jnp
from jax import lax
from jax.experimental import pallas as pl
from jax.experimental.pallas import tpu as pltpu
from jax.sharding import PartitionSpec as P

STEPS = 2
F32 = jnp.float32
BF16 = jnp.bfloat16
LANES = 128
HALF = 64
PIECE = 16
GROUP = 4
MESH = pl.DeviceIdType.MESH


def lane_of(shape):
    return lax.broadcasted_iota(jnp.int32, shape, len(shape) - 1)


def turned(value, by):
    by = by % LANES
    return value if by == 0 else pltpu.roll(value, by, len(value.shape) - 1)


def pack_pair(low, high):
    return jnp.where(lane_of(low.shape) < HALF, low, turned(high, HALF))


def pack_tails(cols):
    out = jnp.zeros_like(cols[0])
    lane = lane_of(out.shape)
    for i, col in enumerate(cols):
        out = jnp.where(lane // PIECE == i, turned(col, PIECE * i - HALF), out)
    return out


def kernel(
    nt, nl, nvar, rows, cols, hid,
    x_ref, loc_ref, val_ref, w1_ref, b1_ref, w2_ref, out_ref,
    xn, xt, base, kept, obs3, bt, pn, pb, rn, rb, en, eb, nu, xb, x3, acc, h3, score,
    qs, rq, st, red1, sum1, red2,
    bar_n_s, bar_n_r, bar_b_s, bar_b_r, edge_s, edge_n_r, edge_b_r, ret_s, ret_r,
    r1_s, r1_r, r2_s, r2_r, w2p, w1s, w2s,
):
    t = lax.axis_index("traj")
    b = lax.axis_index("lon")
    cw = cols // nt
    halo = 2 * STEPS
    ext = cw + 2 * halo
    mt = 5 * cw // 8
    tiles = mt + 6
    count = nt * rows * cols * nl
    lane = lane_of((rows, LANES))
    row = lax.broadcasted_iota(jnp.int32, (rows, LANES), 0)

    def dev(tt, bb):
        return {"traj": lax.rem(tt, nt), "lon": lax.rem(bb, nl)}

    upward = 2 * t < nt

    def nth(i):
        return jnp.where(upward, i, nt - 1 - i)

    own_place = nth(t)

    def other(j):
        return nth(j + jnp.where(j >= own_place, 1, 0))

    barrier = pltpu.get_barrier_semaphore()
    partners = 0
    for db in range(nl):
        for dt in range(nt):
            near = db in (0, 1, nl - 1)
            if (db or dt) and (near or dt == 0):
                pl.semaphore_signal(barrier, inc=1, device_id=dev(t + dt, b + db), device_id_type=MESH)
                partners += 1

    xn[0 : nvar * rows, :] = x_ref[...]
    xn[nvar * rows :, :] = jnp.zeros((LANES * rows - nvar * rows, LANES), F32)

    def flip(r, c):
        xt[pl.ds(r, cols, stride=rows), :] = xn[pl.ds(r, LANES, stride=rows), :].T
        return c

    lax.fori_loop(0, rows, flip, 0, unroll=4)

    def squares(ref, first, n):
        def one(i, c):
            v = ref[pl.ds(first + i * 32, 32), :]
            return c + v * v

        s = lax.fori_loop(0, n // 32, one, jnp.zeros((32, LANES), F32))
        return s[0:8] + s[8:16] + s[16:24] + s[24:32]

    def sum_over_traj(step, part):
        sum1[step, 0] = part
        copies = [
            pltpu.make_async_remote_copy(
                sum1.at[step, 0], red1.at[step, i], r1_s.at[step, i], r1_r.at[step, i],
                device_id=dev(t + i, b), device_id_type=MESH)
            for i in range(1, nt)]
        for cp in copies:
            cp.start()
        return copies

    def sum_over_lon(step, part, copies):
        tot = part
        for i, cp in enumerate(copies):
            cp.wait()
            tot = tot + red1[step, i + 1]
        sum1[step, 1] = tot
        copies = [
            pltpu.make_async_remote_copy(
                sum1.at[step, 1], red2.at[step, i], r2_s.at[step, i], r2_r.at[step, i],
                device_id=dev(t, b + i), device_id_type=MESH)
            for i in range(1, nl)]
        for cp in copies:
            cp.start()
        return tot, copies

    def scale_of(step, tot, copies):
        for i, cp in enumerate(copies):
            cp.wait()
            tot = tot + red2[step, i + 1]
        moment = jnp.sum(tot, axis=0, keepdims=True) / count
        return 1.0 / jnp.sqrt(moment + 1e-06)

    part = squares(xt, 0, cols * rows)
    pl.semaphore_wait(barrier, partners)
    moving = sum_over_traj(0, part)

    obs3[0] = jnp.ones(obs3.shape[1:], F32)
    obs3[0, 0:nvar] = val_ref[:, 0, :]
    full = obs3[0]
    high = full.astype(BF16)
    rest = full - high.astype(F32)
    mid = rest.astype(BF16)
    low = (rest - mid.astype(F32)).astype(BF16)
    three = jnp.concatenate([high, mid, low], 0)
    loc = loc_ref[...]

    def observe(r, c):
        cell = lax.broadcasted_iota(jnp.int32, (cols, loc.shape[1]), 0) + (r * cols * nl + b * cols)
        hot = jnp.where(cell == loc, 1.0, 0.0).astype(BF16)
        o = lax.dot_general(three, hot, (((1,), (1,)), ((), ())), preferred_element_type=F32)
        o = o[0:LANES] + o[LANES : 2 * LANES] + o[2 * LANES :]
        seen = o[nvar : nvar + 1, :] > 0.5
        x = xn[pl.ds(r, LANES, stride=rows), :]
        g = jnp.where(seen, 0.5 * (o - x), 0.0)
        base[pl.ds(r, LANES, stride=rows), :] = jnp.where(seen, 0.5 * (x + g + o), x)
        bt[pl.ds(r, cols, stride=rows), :] = (x + g).T
        return c

    lax.fori_loop(0, rows, observe, 0, unroll=2)
    part, moving = sum_over_lon(0, part, moving)

    wide = 2 * LANES
    deep = 3 * nvar
    w2p[deep // PIECE * PIECE :, :] = jnp.zeros((wide - deep // PIECE * PIECE, w2p.shape[1]), BF16)
    w2p[0:deep, :] = w2_ref[...]
    for a in range(3):
        for k in range(3):
            tap, to = 3 * a + k, 3 * k + a
            w1s[(to + 1) * wide - 2 * PIECE : (to + 1) * wide, :] = jnp.zeros((2 * PIECE, hid), BF16)
            w1s[to * wide : to * wide + deep, :] = w1_ref[tap * deep : (tap + 1) * deep, :]
            v = w2p[:, tap * hid : (tap + 1) * hid].astype(F32)
            w2s[to * hid : (to + 1) * hid, :] = v.T.astype(BF16)

    scale = scale_of(0, part, moving)

    def tiled(value):
        return value.reshape(-1, rows, LANES)

    def flat(value):
        return value.reshape(-1, LANES)

    def pack_main(get, put):
        step = cw // 8
        for i in range(4):
            put(i * step, pack_pair(get(i * step, step), get(cw // 2 + i * step, step)))
        put(cw // 2, pack_tails([get(step * i, step) for i in range(8)]))

    def pack_all(get, dest):
        zero = jnp.zeros((3, rows, LANES), BF16)
        dest[1, 0:3] = zero
        dest[nt, tiles - 3 :] = zero

        def sub(k, carry):
            def put(j, v):
                dest[k + 1, pl.ds(3 + j, v.shape[0] // rows)] = tiled(v.astype(BF16))

            pack_main(lambda c, n: get(k * cw + c, n), put)
            for first, slot, at in ((k * cw, k, tiles - 3), (k * cw + cw - halo, k + 2, 0)):
                dest[slot, at : at + 2] = tiled(pack_pair(get(first, 2), get(first + 2, 2)).astype(BF16))
                dest[slot, at + 2] = pack_tails([get(first + i, 1) for i in range(4)]).astype(BF16)
            return carry

        lax.fori_loop(0, nt, sub, 0)

    def send_all(src, dst, edge, s_sem, r_sem, e_sem, f):
        right = pltpu.make_async_remote_copy(
            src.at[nt + 1, 0:3], edge.at[t], edge_s.at[f, 0], e_sem.at[t],
            device_id=dev(0, b + 1), device_id_type=MESH)
        left = pltpu.make_async_remote_copy(
            src.at[0, tiles - 3 : tiles], edge.at[t], edge_s.at[f, 1], e_sem.at[t],
            device_id=dev(nt - 1, b + nl - 1), device_id_type=MESH)
        right.start()
        left.start()
        copies = [right, left]
        for j in range(nt - 1):
            k = other(j)
            cp = pltpu.make_async_remote_copy(
                src.at[k + 1], dst.at[t], s_sem.at[j], r_sem.at[t],
                device_id=dev(k, b), device_id_type=MESH)
            cp.start()
            copies.append(cp)
        dst[t] = src[t + 1]
        return copies

    def receive(s, src, dst, edge, s_sem, r_sem, e_sem, f):
        @pl.when(s != t)
        def _():
            pltpu.make_async_remote_copy(
                src.at[s + 1], dst.at[s], s_sem.at[0], r_sem.at[s],
                device_id=dev(s, b), device_id_type=MESH).wait_recv()

        def edges(at):
            pltpu.make_async_remote_copy(
                src.at[0, 0:3], edge.at[s], edge_s.at[f, 0], e_sem.at[s],
                device_id=dev(0, b + 1), device_id_type=MESH).wait_recv()
            dst[s, at : at + 3] = edge[s]

        @pl.when(t == 0)
        def _():
            edges(0)

        @pl.when(t == nt - 1)
        def _():
            edges(tiles - 3)

    def unpack_main(tile, put):
        step = cw // 8
        tail = tile(cw // 2, step)
        for i in range(8):
            a = turned(tile((i % 4) * step, step), HALF * (i // 4))
            put(i * step, jnp.where(lane_of(a.shape) < HALF, a, turned(tail, HALF - PIECE * i)))

    def unpack_state(s, src, put):
        def tile(j, n):
            return flat(src[s, pl.ds(j, n)].astype(F32))

        for at, first in ((0, 0), (tiles - 3, cw + halo)):
            pairs = tile(at, 2)
            tail = tile(at + 2, 1)
            for i in range(4):
                a = turned(pairs[(i % 2) * rows : (i % 2 + 1) * rows], HALF * (i // 2))
                put(s, first + i, jnp.where(lane < HALF, a, turned(tail, HALF - PIECE * i)))
        unpack_main(lambda j, n: tile(3 + j, n), lambda c, v: put(s, c + halo, v))

    pack_all(lambda c, n: xt[pl.ds(c * rows, n * rows), :] * scale, pn)
    sent_n = send_all(pn, rn, en, bar_n_s, bar_n_r, edge_n_r, 0)

    pack_all(lambda c, n: bt[pl.ds(c * rows, n * rows), :], pb)
    sent_b = send_all(pb, rb, eb, bar_b_s, bar_b_r, edge_b_r, 1)

    acc[0] = jnp.zeros(acc.shape[1:], F32)
    acc[nt + 1] = jnp.zeros(acc.shape[1:], F32)
    nu[0] = jnp.zeros(nu.shape[1:], F32)
    nu[nt + 1] = jnp.zeros(nu.shape[1:], F32)

    def put_n(s, c, v):
        nu[s + 1, pl.ds(c, v.shape[0] // rows)] = tiled(v)

    def arrive(s):
        receive(s, pn, rn, en, bar_n_s, bar_n_r, edge_n_r, 0)
        unpack_state(s, rn, put_n)

    def spread(dest, c, tile_list):
        n = len(tile_list)
        many = tile_list[0].shape[0]
        rown = lax.broadcasted_iota(jnp.int32, (many, LANES), 0) % rows
        for i, v in enumerate(tile_list):
            up = jnp.where(rown == 0, 0.0, pltpu.roll(v, 1, 0))
            down = jnp.where(rown == rows - 1, 0.0, pltpu.roll(v, many - 1, 0))
            for a, piece in enumerate((up, v, down)):
                dest[pl.ds(c, many // rows), :, a * n * LANES + i * LANES : a * n * LANES + (i + 1) * LANES] = tiled(
                    piece.astype(BF16))

    two = 2 * nvar - LANES

    def combine(s, wid):
        def share(j, k):
            at = pl.ds(j * GROUP * rows, GROUP * rows)
            above = acc[s + 2, at, 0:LANES]
            c0 = acc[s + 1, at, 0:LANES]
            c1 = acc[s + 1, at, LANES : 2 * LANES]
            below = acc[s, at, LANES : 2 * LANES]
            here = turned(jnp.where(lane_of(c0.shape) >= nvar, c0, c1), -nvar)
            score[s + 1, pl.ds(j * GROUP, GROUP)] = tiled(here + above + turned(below, -two))
            return k

        lax.fori_loop(0, wid // GROUP, share, 0, unroll=2 if wid // GROUP % 2 == 0 else 1)

    def give_back(s):
        def get(c, n):
            return flat(0.5 * score[s + 1, pl.ds(c, n)] + kept[s, pl.ds(c + 2, n)])

        def put(j, v):
            qs[s, pl.ds(j, v.shape[0] // rows)] = tiled(v.astype(BF16))

        pack_main(get, put)

        @pl.when(s != t)
        def _():
            pltpu.make_async_remote_copy(
                qs.at[s], rq.at[t], ret_s.at[s], ret_r.at[t],
                device_id=dev(s, b), device_id_type=MESH).start()

        @pl.when(s == t)
        def _():
            rq[t] = qs[s]

    def network(width, step):
        def state(i, carry):
            s = nth(i) if step == 0 else nth(nt - 1 - i)
            if step == 0:
                @pl.when(i < nt - 1)
                def _():
                    arrive(nth(i + 1))

            def window(j, k):
                c = j * GROUP
                before, here, after = [flat(nu[s + i, pl.ds(c, GROUP)]) for i in range(3)]
                lane = lane_of(here.shape)
                moved = turned(here, nvar)
                first = jnp.where(lane < nvar, before, moved)
                last = jnp.where(lane < two, moved, jnp.where(lane < two + nvar, turned(after, two), 0.0))
                spread(x3, c, [first, last])
                return k

            lax.fori_loop(0, width // GROUP, window, 0, unroll=2)
            wid = width - 2
            bias = b1_ref[...]
            chunk = wid // 2
            for start in range(0, wid, chunk):
                lhs = jnp.concatenate(
                    [x3[start + k : start + k + chunk].reshape(chunk * rows, 3 * wide) for k in range(3)], 1)
                whole = jnp.dot(lhs, w1s[...], preferred_element_type=F32)
                for c in range(0, chunk, GROUP):
                    n = min(GROUP, chunk - c)
                    v = whole[c * rows : (c + n) * rows] + bias
                    v = 0.5 * v
                    v = v + v * jnp.tanh(v)
                    v = v.astype(BF16).astype(F32)
                    spread(h3, start + c, [v[:, m * LANES : (m + 1) * LANES] for m in range(hid // LANES)])
            wid = width - 4
            lhs = jnp.concatenate(
                [h3[k : k + wid].reshape(wid * rows, 3 * hid) for k in range(3)], 1)
            acc[s + 1, 0 : wid * rows, :] = jnp.dot(lhs, w2s[...], preferred_element_type=F32)

            @pl.when(i > 0)
            def _():
                done = nth(i - 1) if step == 0 else nth(nt - i)
                combine(done, width - 4)
                if step:
                    give_back(done)

            return carry

        lax.fori_loop(0, nt, state, 0)
        done = nth(nt - 1) if step == 0 else nth(0)
        combine(done, width - 4)
        if step:
            give_back(done)

    def take_back():
        for i in range(1, nt):
            k = lax.rem(t + i, nt)
            pltpu.make_async_remote_copy(
                qs.at[k], rq.at[k], ret_s.at[k], ret_r.at[k],
                device_id=dev(k, b), device_id_type=MESH).wait_recv()

        def band(k, carry):
            def put(c, v):
                st[pl.ds((k * cw + c) * rows, v.shape[0]), :] = v

            unpack_main(lambda j, n: flat(rq[k, pl.ds(j, n)].astype(F32)), put)
            return carry

        lax.fori_loop(0, nt, band, 0)

    arrive(nth(0))
    network(ext, 0)


    def put_x(s, c, v):
        xb[s, pl.ds(c, v.shape[0] // rows)] = tiled(v)

    def arrive_base(i, carry):
        s = nth(i)
        receive(s, pb, rb, eb, bar_b_s, bar_b_r, edge_b_r, 1)
        unpack_state(s, rb, put_x)
        return carry

    lax.fori_loop(0, nt, arrive_base, 0)

    def advance(s, total):
        def one(j, k):
            at = pl.ds(j * GROUP, GROUP)
            here = flat(xb[s, pl.ds(j * GROUP + 2, GROUP)])
            change = flat(score[s + 1, at])
            nu[s + 1, at] = tiled(here + 0.5 * change)
            kept[s, at] = tiled((0.5 - 0.5 * here[:, nvar : nvar + 1]) * change)
            return k

        lax.fori_loop(0, (ext - 4) // GROUP, one, 0)

        def sq(c, k):
            v = nu[s + 1, c + 2]
            return k + v * v

        return lax.fori_loop(0, cw, sq, total, unroll=2)

    total = lax.fori_loop(0, nt, advance, jnp.zeros((rows, LANES), F32))
    part = total[0:8]
    for i in range(1, rows // 8):
        part = part + total[8 * i : 8 * i + 8]
    moving = sum_over_traj(1, part)
    part, moving = sum_over_lon(1, part, moving)
    scale = scale_of(1, part, moving)

    def rescale(s, carry):
        def one(j, k):
            at = pl.ds(j * GROUP, GROUP)
            nu[s + 1, at] = (nu[s + 1, at] * scale).astype(BF16).astype(F32)
            return k

        return lax.fori_loop(0, (ext - 4) // GROUP, one, carry)

    lax.fori_loop(0, nt, rescale, 0)
    network(ext - 4, 1)

    take_back()

    def add_second(r, c):
        v = st[pl.ds(r, cols, stride=rows), :].T
        at = pl.ds(r, LANES, stride=rows)
        base[at, :] = base[at, :] + v
        return c

    lax.fori_loop(0, rows, add_second, 0, unroll=4)
    out_ref[...] = base[0 : nvar * rows, :]
    for cp in sent_n + sent_b:
        cp.wait_send()
    for i in range(1, nt):
        k = lax.rem(t + i, nt)
        pltpu.make_async_remote_copy(
            qs.at[k], rq.at[t], ret_s.at[k], ret_r.at[t],
            device_id=dev(k, b), device_id_type=MESH).wait_send()


def body(states, obs_index, obs_values, first_weight, first_bias, second_weight):
    nt, nl = lax.axis_size("traj"), lax.axis_size("lon")
    _, nvar, rows, cols = states.shape
    hid = first_bias.shape[0]
    wide = 2 * LANES
    cw = cols // nt
    ext = cw + 4 * STEPS
    mt = 5 * cw // 8
    tiles = mt + 6
    nobs = obs_values.shape[2]
    dma = pltpu.SemaphoreType.DMA
    vm = pltpu.VMEM
    big = LANES * rows
    scratch = [
        vm((big, LANES), F32), vm((cols * rows, LANES), F32), vm((big, LANES), F32), vm((nt, ext - 4, rows, LANES), F32),
        vm((1, LANES, nobs), F32), vm((cols * rows, LANES), F32),
        vm((nt + 2, tiles, rows, LANES), BF16), vm((nt + 2, tiles, rows, LANES), BF16),
        vm((nt, tiles, rows, LANES), BF16), vm((nt, tiles, rows, LANES), BF16),
        vm((nt, 3, rows, LANES), BF16), vm((nt, 3, rows, LANES), BF16),
        vm((nt + 2, ext, rows, LANES), F32), vm((nt, ext, rows, LANES), F32),
        vm((ext, rows, 3 * wide), BF16), vm((nt + 2, (ext - 4) * rows, wide), F32), vm((ext, rows, 3 * hid), BF16),
        vm((nt + 2, ext - 4, rows, LANES), F32),
        vm((nt, mt, rows, LANES), BF16), vm((nt, mt, rows, LANES), BF16),
        vm((cols * rows, LANES), F32),
        vm((STEPS, nt, 8, LANES), F32), vm((STEPS, 2, 8, LANES), F32), vm((STEPS, nl, 8, LANES), F32),
        dma((nt,)), dma((nt,)), dma((nt,)), dma((nt,)), dma((2, 2)), dma((nt,)), dma((nt,)),
        dma((nt,)), dma((nt,)),
        dma((STEPS, nt)), dma((STEPS, nt)), dma((STEPS, nl)), dma((STEPS, nl)),
        vm((wide, 9 * hid), BF16), vm((9 * wide, hid), BF16), vm((9 * hid, wide), BF16),
    ]
    out = pl.pallas_call(
        functools.partial(kernel, nt, nl, nvar, rows, cols, hid),
        out_shape=jax.ShapeDtypeStruct((nvar * rows, cols), F32),
        in_specs=[pl.BlockSpec(memory_space=vm)] * 6,
        out_specs=pl.BlockSpec(memory_space=vm),
        scratch_shapes=scratch,
        compiler_params=pltpu.CompilerParams(
            collective_id=0, has_side_effects=True, vmem_limit_bytes=60 << 20),
    )(states.reshape(nvar * rows, cols), obs_index, obs_values.reshape(nvar, 1, nobs), first_weight.T, first_bias.reshape(1, hid), second_weight)
    return out.reshape(1, nvar, rows, cols)


def solution(mesh):
    placed = (P("traj", None, None, "lon"), P("traj", "lon"), P("traj", None, "lon"), P(), P(), P())
    return jax.shard_map(
        body, mesh=mesh, in_specs=placed, out_specs=P("traj", None, None, "lon"), check_vma=False
    )
```

```python
import functools

import jax
import jax.numpy as jnp
from jax import lax
from jax.experimental import pallas as pl
from jax.experimental.pallas import tpu as pltpu
from jax.sharding import PartitionSpec as P

STEPS = 2
F32 = jnp.float32
BF16 = jnp.bfloat16
LANES = 128
HALF = 64
PIECE = 16
GROUP = 4
MESH = pl.DeviceIdType.MESH


def lane_of(shape):
    return lax.broadcasted_iota(jnp.int32, shape, len(shape) - 1)


def turned(value, by):
    by = by % LANES
    return value if by == 0 else pltpu.roll(value, by, len(value.shape) - 1)


def pack_pair(low, high):
    return jnp.where(lane_of(low.shape) < HALF, low, turned(high, HALF))


def pack_tails(cols):
    out = jnp.zeros_like(cols[0])
    lane = lane_of(out.shape)
    for i, col in enumerate(cols):
        out = jnp.where(lane // PIECE == i, turned(col, PIECE * i - HALF), out)
    return out


def kernel(
    nt, nl, nvar, rows, cols, hid,
    x_ref, loc_ref, val_ref, w1_ref, b1_ref, w2_ref, out_ref,
    xn, xt, base, kept, obs3, bt, pn, pb, rn, rb, en, eb, nu, xb, x3, acc, h3, score,
    qs, rq, st, red1, sum1, red2,
    bar_n_s, bar_n_r, bar_b_s, bar_b_r, edge_s, edge_n_r, edge_b_r, ret_s, ret_r,
    r1_s, r1_r, r2_s, r2_r, w2p, w1s, w2s,
):
    t = lax.axis_index("traj")
    b = lax.axis_index("lon")
    cw = cols // nt
    halo = 2 * STEPS
    ext = cw + 2 * halo
    mt = 5 * cw // 8
    tiles = mt + 6
    count = nt * rows * cols * nl
    lane = lane_of((rows, LANES))
    row = lax.broadcasted_iota(jnp.int32, (rows, LANES), 0)

    def dev(tt, bb):
        return {"traj": lax.rem(tt, nt), "lon": lax.rem(bb, nl)}

    upward = 2 * t < nt

    def nth(i):
        return jnp.where(upward, i, nt - 1 - i)

    own_place = nth(t)

    def other(j):
        return nth(j + jnp.where(j >= own_place, 1, 0))

    barrier = pltpu.get_barrier_semaphore()
    partners = 0
    for db in range(nl):
        for dt in range(nt):
            near = db in (0, 1, nl - 1)
            if (db or dt) and (near or dt == 0):
                pl.semaphore_signal(barrier, inc=1, device_id=dev(t + dt, b + db), device_id_type=MESH)
                partners += 1

    xn[0 : nvar * rows, :] = x_ref[...]
    xn[nvar * rows :, :] = jnp.zeros((LANES * rows - nvar * rows, LANES), F32)

    def flip(r, c):
        xt[pl.ds(r, cols, stride=rows), :] = xn[pl.ds(r, LANES, stride=rows), :].T
        return c

    lax.fori_loop(0, rows, flip, 0, unroll=4)

    def squares(ref, first, n):
        def one(i, c):
            v = ref[pl.ds(first + i * 32, 32), :]
            return c + v * v

        s = lax.fori_loop(0, n // 32, one, jnp.zeros((32, LANES), F32))
        return s[0:8] + s[8:16] + s[16:24] + s[24:32]

    def sum_over_traj(step, part):
        sum1[step, 0] = part
        copies = [
            pltpu.make_async_remote_copy(
                sum1.at[step, 0], red1.at[step, i], r1_s.at[step, i], r1_r.at[step, i],
                device_id=dev(t + i, b), device_id_type=MESH)
            for i in range(1, nt)]
        for cp in copies:
            cp.start()
        return copies

    def sum_over_lon(step, part, copies):
        tot = part
        for i, cp in enumerate(copies):
            cp.wait()
            tot = tot + red1[step, i + 1]
        sum1[step, 1] = tot
        copies = [
            pltpu.make_async_remote_copy(
                sum1.at[step, 1], red2.at[step, i], r2_s.at[step, i], r2_r.at[step, i],
                device_id=dev(t, b + i), device_id_type=MESH)
            for i in range(1, nl)]
        for cp in copies:
            cp.start()
        return tot, copies

    def scale_of(step, tot, copies):
        for i, cp in enumerate(copies):
            cp.wait()
            tot = tot + red2[step, i + 1]
        moment = jnp.sum(tot, axis=0, keepdims=True) / count
        return 1.0 / jnp.sqrt(moment + 1e-06)

    part = squares(xt, 0, cols * rows)
    pl.semaphore_wait(barrier, partners)
    moving = sum_over_traj(0, part)

    obs3[0] = jnp.ones(obs3.shape[1:], F32)
    obs3[0, 0:nvar] = val_ref[:, 0, :]
    full = obs3[0]
    high = full.astype(BF16)
    rest = full - high.astype(F32)
    mid = rest.astype(BF16)
    low = (rest - mid.astype(F32)).astype(BF16)
    three = jnp.concatenate([high, mid, low], 0)
    loc = loc_ref[...]

    def observe(r, c):
        cell = lax.broadcasted_iota(jnp.int32, (cols, loc.shape[1]), 0) + (r * cols * nl + b * cols)
        hot = jnp.where(cell == loc, 1.0, 0.0).astype(BF16)
        o = lax.dot_general(three, hot, (((1,), (1,)), ((), ())), preferred_element_type=F32)
        o = o[0:LANES] + o[LANES : 2 * LANES] + o[2 * LANES :]
        seen = o[nvar : nvar + 1, :] > 0.5
        x = xn[pl.ds(r, LANES, stride=rows), :]
        g = jnp.where(seen, 0.5 * (o - x), 0.0)
        base[pl.ds(r, LANES, stride=rows), :] = jnp.where(seen, 0.5 * (x + g + o), x)
        bt[pl.ds(r, cols, stride=rows), :] = (x + g).T
        return c

    lax.fori_loop(0, rows, observe, 0, unroll=2)
    part, moving = sum_over_lon(0, part, moving)

    wide = 2 * LANES
    deep = 3 * nvar
    w2p[deep // PIECE * PIECE :, :] = jnp.zeros((wide - deep // PIECE * PIECE, w2p.shape[1]), BF16)
    w2p[0:deep, :] = w2_ref[...]
    for a in range(3):
        for k in range(3):
            tap, to = 3 * a + k, 3 * k + a
            w1s[(to + 1) * wide - 2 * PIECE : (to + 1) * wide, :] = jnp.zeros((2 * PIECE, hid), BF16)
            w1s[to * wide : to * wide + deep, :] = w1_ref[tap * deep : (tap + 1) * deep, :]
            v = w2p[:, tap * hid : (tap + 1) * hid].astype(F32)
            w2s[to * hid : (to + 1) * hid, :] = v.T.astype(BF16)

    scale = scale_of(0, part, moving)

    def tiled(value):
        return value.reshape(-1, rows, LANES)

    def flat(value):
        return value.reshape(-1, LANES)

    def pack_main(get, put):
        step = cw // 8
        for i in range(4):
            put(i * step, pack_pair(get(i * step, step), get(cw // 2 + i * step, step)))
        put(cw // 2, pack_tails([get(step * i, step) for i in range(8)]))

    def pack_all(get, dest):
        zero = jnp.zeros((3, rows, LANES), BF16)
        dest[1, 0:3] = zero
        dest[nt, tiles - 3 :] = zero

        def sub(k, carry):
            def put(j, v):
                dest[k + 1, pl.ds(3 + j, v.shape[0] // rows)] = tiled(v.astype(BF16))

            pack_main(lambda c, n: get(k * cw + c, n), put)
            for first, slot, at in ((k * cw, k, tiles - 3), (k * cw + cw - halo, k + 2, 0)):
                dest[slot, at : at + 2] = tiled(pack_pair(get(first, 2), get(first + 2, 2)).astype(BF16))
                dest[slot, at + 2] = pack_tails([get(first + i, 1) for i in range(4)]).astype(BF16)
            return carry

        lax.fori_loop(0, nt, sub, 0)

    def send_all(src, dst, edge, s_sem, r_sem, e_sem, f):
        right = pltpu.make_async_remote_copy(
            src.at[nt + 1, 0:3], edge.at[t], edge_s.at[f, 0], e_sem.at[t],
            device_id=dev(0, b + 1), device_id_type=MESH)
        left = pltpu.make_async_remote_copy(
            src.at[0, tiles - 3 : tiles], edge.at[t], edge_s.at[f, 1], e_sem.at[t],
            device_id=dev(nt - 1, b + nl - 1), device_id_type=MESH)
        right.start()
        left.start()
        copies = [right, left]
        for j in range(nt - 1):
            k = other(j)
            cp = pltpu.make_async_remote_copy(
                src.at[k + 1], dst.at[t], s_sem.at[j], r_sem.at[t],
                device_id=dev(k, b), device_id_type=MESH)
            cp.start()
            copies.append(cp)
        dst[t] = src[t + 1]
        return copies

    def receive(s, src, dst, edge, s_sem, r_sem, e_sem, f):
        @pl.when(s != t)
        def _():
            pltpu.make_async_remote_copy(
                src.at[s + 1], dst.at[s], s_sem.at[0], r_sem.at[s],
                device_id=dev(s, b), device_id_type=MESH).wait_recv()

        def edges(at):
            pltpu.make_async_remote_copy(
                src.at[0, 0:3], edge.at[s], edge_s.at[f, 0], e_sem.at[s],
                device_id=dev(0, b + 1), device_id_type=MESH).wait_recv()
            dst[s, at : at + 3] = edge[s]

        @pl.when(t == 0)
        def _():
            edges(0)

        @pl.when(t == nt - 1)
        def _():
            edges(tiles - 3)

    def unpack_main(tile, put):
        step = cw // 8
        tail = tile(cw // 2, step)
        for i in range(8):
            a = turned(tile((i % 4) * step, step), HALF * (i // 4))
            put(i * step, jnp.where(lane_of(a.shape) < HALF, a, turned(tail, HALF - PIECE * i)))

    def unpack_state(s, src, put):
        def tile(j, n):
            return flat(src[s, pl.ds(j, n)].astype(F32))

        for at, first in ((0, 0), (tiles - 3, cw + halo)):
            pairs = tile(at, 2)
            tail = tile(at + 2, 1)
            for i in range(4):
                a = turned(pairs[(i % 2) * rows : (i % 2 + 1) * rows], HALF * (i // 2))
                put(s, first + i, jnp.where(lane < HALF, a, turned(tail, HALF - PIECE * i)))
        unpack_main(lambda j, n: tile(3 + j, n), lambda c, v: put(s, c + halo, v))

    pack_all(lambda c, n: xt[pl.ds(c * rows, n * rows), :] * scale, pn)
    sent_n = send_all(pn, rn, en, bar_n_s, bar_n_r, edge_n_r, 0)

    pack_all(lambda c, n: bt[pl.ds(c * rows, n * rows), :], pb)
    sent_b = send_all(pb, rb, eb, bar_b_s, bar_b_r, edge_b_r, 1)

    acc[0] = jnp.zeros(acc.shape[1:], F32)
    acc[nt + 1] = jnp.zeros(acc.shape[1:], F32)
    nu[0] = jnp.zeros(nu.shape[1:], F32)
    nu[nt + 1] = jnp.zeros(nu.shape[1:], F32)

    def put_n(s, c, v):
        nu[s + 1, pl.ds(c, v.shape[0] // rows)] = tiled(v)

    def arrive(s):
        receive(s, pn, rn, en, bar_n_s, bar_n_r, edge_n_r, 0)
        unpack_state(s, rn, put_n)

    def spread(dest, c, tile_list):
        n = len(tile_list)
        many = tile_list[0].shape[0]
        rown = lax.broadcasted_iota(jnp.int32, (many, LANES), 0) % rows
        for i, v in enumerate(tile_list):
            up = jnp.where(rown == 0, 0.0, pltpu.roll(v, 1, 0))
            down = jnp.where(rown == rows - 1, 0.0, pltpu.roll(v, many - 1, 0))
            for a, piece in enumerate((up, v, down)):
                dest[pl.ds(c, many // rows), :, a * n * LANES + i * LANES : a * n * LANES + (i + 1) * LANES] = tiled(
                    piece.astype(BF16))

    two = 2 * nvar - LANES

    def combine(s, wid):
        def share(j, k):
            at = pl.ds(j * GROUP * rows, GROUP * rows)
            above = acc[s + 2, at, 0:LANES]
            c0 = acc[s + 1, at, 0:LANES]
            c1 = acc[s + 1, at, LANES : 2 * LANES]
            below = acc[s, at, LANES : 2 * LANES]
            here = turned(jnp.where(lane_of(c0.shape) >= nvar, c0, c1), -nvar)
            score[s + 1, pl.ds(j * GROUP, GROUP)] = tiled(here + above + turned(below, -two))
            return k

        lax.fori_loop(0, wid // GROUP, share, 0, unroll=2 if wid // GROUP % 2 == 0 else 1)

    def give_back(s):
        def get(c, n):
            return flat(0.5 * score[s + 1, pl.ds(c, n)] + kept[s, pl.ds(c + 2, n)])

        def put(j, v):
            qs[s, pl.ds(j, v.shape[0] // rows)] = tiled(v.astype(BF16))

        pack_main(get, put)

        @pl.when(s != t)
        def _():
            pltpu.make_async_remote_copy(
                qs.at[s], rq.at[t], ret_s.at[s], ret_r.at[t],
                device_id=dev(s, b), device_id_type=MESH).start()

        @pl.when(s == t)
        def _():
            rq[t] = qs[s]

    def network(width, step):
        def state(i, carry):
            s = nth(i) if step == 0 else nth(nt - 1 - i)
            if step == 0:
                @pl.when(i < nt - 1)
                def _():
                    arrive(nth(i + 1))

            def window(c):
                before, here, after = [flat(nu[s + i, pl.ds(c, GROUP)]) for i in range(3)]
                lane = lane_of(here.shape)
                moved = turned(here, nvar)
                first = jnp.where(lane < nvar, before, moved)
                last = jnp.where(lane < two, moved, jnp.where(lane < two + nvar, turned(after, two), 0.0))
                spread(x3, c, [first, last])

            built = 0
            wid = width - 2
            bias = b1_ref[...]
            chunk = wid // 2
            for start in range(0, wid, chunk):
                while built < start + chunk + 2:
                    window(built)
                    built += GROUP
                lhs = jnp.concatenate(
                    [x3[start + k : start + k + chunk].reshape(chunk * rows, 3 * wide) for k in range(3)], 1)
                whole = jnp.dot(lhs, w1s[...], preferred_element_type=F32)
                for c in range(0, chunk, GROUP):
                    n = min(GROUP, chunk - c)
                    v = whole[c * rows : (c + n) * rows] + bias
                    v = 0.5 * v
                    v = v + v * jnp.tanh(v)
                    v = v.astype(BF16).astype(F32)
                    spread(h3, start + c, [v[:, m * LANES : (m + 1) * LANES] for m in range(hid // LANES)])
            wid = width - 4
            chunk = wid // 2
            for start in range(0, wid, chunk):
                lhs = jnp.concatenate(
                    [h3[start + k : start + k + chunk].reshape(chunk * rows, 3 * hid) for k in range(3)], 1)
                acc[s + 1, start * rows : (start + chunk) * rows, :] = jnp.dot(
                    lhs, w2s[...], preferred_element_type=F32)

            @pl.when(i > 0)
            def _():
                done = nth(i - 1) if step == 0 else nth(nt - i)
                combine(done, width - 4)
                if step:
                    give_back(done)

            return carry

        lax.fori_loop(0, nt, state, 0)
        done = nth(nt - 1) if step == 0 else nth(0)
        combine(done, width - 4)
        if step:
            give_back(done)

    def take_back():
        for i in range(1, nt):
            k = lax.rem(t + i, nt)
            pltpu.make_async_remote_copy(
                qs.at[k], rq.at[k], ret_s.at[k], ret_r.at[k],
                device_id=dev(k, b), device_id_type=MESH).wait_recv()

        def band(k, carry):
            def put(c, v):
                st[pl.ds((k * cw + c) * rows, v.shape[0]), :] = v

            unpack_main(lambda j, n: flat(rq[k, pl.ds(j, n)].astype(F32)), put)
            return carry

        lax.fori_loop(0, nt, band, 0)

    arrive(nth(0))
    network(ext, 0)


    def put_x(s, c, v):
        xb[s, pl.ds(c, v.shape[0] // rows)] = tiled(v)

    def arrive_base(i, carry):
        s = nth(i)
        receive(s, pb, rb, eb, bar_b_s, bar_b_r, edge_b_r, 1)
        unpack_state(s, rb, put_x)
        return carry

    lax.fori_loop(0, nt, arrive_base, 0)

    def advance(s, total):
        def one(j, k):
            at = pl.ds(j * GROUP, GROUP)
            here = flat(xb[s, pl.ds(j * GROUP + 2, GROUP)])
            change = flat(score[s + 1, at])
            nu[s + 1, at] = tiled(here + 0.5 * change)
            kept[s, at] = tiled((0.5 - 0.5 * here[:, nvar : nvar + 1]) * change)
            return k

        lax.fori_loop(0, (ext - 4) // GROUP, one, 0)

        def sq(c, k):
            v = nu[s + 1, c + 2]
            return k + v * v

        return lax.fori_loop(0, cw, sq, total, unroll=2)

    total = lax.fori_loop(0, nt, advance, jnp.zeros((rows, LANES), F32))
    part = total[0:8]
    for i in range(1, rows // 8):
        part = part + total[8 * i : 8 * i + 8]
    moving = sum_over_traj(1, part)
    part, moving = sum_over_lon(1, part, moving)
    scale = scale_of(1, part, moving)

    def rescale(s, carry):
        def one(j, k):
            at = pl.ds(j * GROUP, GROUP)
            nu[s + 1, at] = (nu[s + 1, at] * scale).astype(BF16).astype(F32)
            return k

        return lax.fori_loop(0, (ext - 4) // GROUP, one, carry)

    lax.fori_loop(0, nt, rescale, 0)
    network(ext - 4, 1)

    take_back()

    def add_second(r, c):
        v = st[pl.ds(r, cols, stride=rows), :].T
        at = pl.ds(r, LANES, stride=rows)
        base[at, :] = base[at, :] + v
        return c

    lax.fori_loop(0, rows, add_second, 0, unroll=4)
    out_ref[...] = base[0 : nvar * rows, :]
    for cp in sent_n + sent_b:
        cp.wait_send()
    for i in range(1, nt):
        k = lax.rem(t + i, nt)
        pltpu.make_async_remote_copy(
            qs.at[k], rq.at[t], ret_s.at[k], ret_r.at[t],
            device_id=dev(k, b), device_id_type=MESH).wait_send()


def body(states, obs_index, obs_values, first_weight, first_bias, second_weight):
    nt, nl = lax.axis_size("traj"), lax.axis_size("lon")
    _, nvar, rows, cols = states.shape
    hid = first_bias.shape[0]
    wide = 2 * LANES
    cw = cols // nt
    ext = cw + 4 * STEPS
    mt = 5 * cw // 8
    tiles = mt + 6
    nobs = obs_values.shape[2]
    dma = pltpu.SemaphoreType.DMA
    vm = pltpu.VMEM
    big = LANES * rows
    scratch = [
        vm((big, LANES), F32), vm((cols * rows, LANES), F32), vm((big, LANES), F32), vm((nt, ext - 4, rows, LANES), F32),
        vm((1, LANES, nobs), F32), vm((cols * rows, LANES), F32),
        vm((nt + 2, tiles, rows, LANES), BF16), vm((nt + 2, tiles, rows, LANES), BF16),
        vm((nt, tiles, rows, LANES), BF16), vm((nt, tiles, rows, LANES), BF16),
        vm((nt, 3, rows, LANES), BF16), vm((nt, 3, rows, LANES), BF16),
        vm((nt + 2, ext, rows, LANES), F32), vm((nt, ext, rows, LANES), F32),
        vm((ext, rows, 3 * wide), BF16), vm((nt + 2, (ext - 4) * rows, wide), F32), vm((ext, rows, 3 * hid), BF16),
        vm((nt + 2, ext - 4, rows, LANES), F32),
        vm((nt, mt, rows, LANES), BF16), vm((nt, mt, rows, LANES), BF16),
        vm((cols * rows, LANES), F32),
        vm((STEPS, nt, 8, LANES), F32), vm((STEPS, 2, 8, LANES), F32), vm((STEPS, nl, 8, LANES), F32),
        dma((nt,)), dma((nt,)), dma((nt,)), dma((nt,)), dma((2, 2)), dma((nt,)), dma((nt,)),
        dma((nt,)), dma((nt,)),
        dma((STEPS, nt)), dma((STEPS, nt)), dma((STEPS, nl)), dma((STEPS, nl)),
        vm((wide, 9 * hid), BF16), vm((9 * wide, hid), BF16), vm((9 * hid, wide), BF16),
    ]
    out = pl.pallas_call(
        functools.partial(kernel, nt, nl, nvar, rows, cols, hid),
        out_shape=jax.ShapeDtypeStruct((nvar * rows, cols), F32),
        in_specs=[pl.BlockSpec(memory_space=vm)] * 6,
        out_specs=pl.BlockSpec(memory_space=vm),
        scratch_shapes=scratch,
        compiler_params=pltpu.CompilerParams(
            collective_id=0, has_side_effects=True, vmem_limit_bytes=60 << 20),
    )(states.reshape(nvar * rows, cols), obs_index, obs_values.reshape(nvar, 1, nobs), first_weight.T, first_bias.reshape(1, hid), second_weight)
    return out.reshape(1, nvar, rows, cols)


def solution(mesh):
    placed = (P("traj", None, None, "lon"), P("traj", "lon"), P("traj", None, "lon"), P(), P(), P())
    return jax.shard_map(
        body, mesh=mesh, in_specs=placed, out_specs=P("traj", None, None, "lon"), check_vma=False
    )
```
